32 devices in a mesh: ha: 4 (over y, x), wa: 8 (over z, core).
Axes of the slice: x: 2, y: 2, z: 4, core: 2. Of those that a mesh axis runs over, the one named last changes fastest.
Arguments:
- inputs: bfloat16 [32, 8, 16, 1536], P(None, 'ha', 'wa'), may hold values from -6 to 6
- query_vectors: bfloat16 [32, 8, 16, 1536], P(None, 'ha', 'wa'), may hold values from -256 to 256
- key_vectors: bfloat16 [32, 8, 16, 1536], P(None, 'ha', 'wa'), may hold values from -32 to 32
- value_vectors: bfloat16 [32, 8, 16, 1536], P(None, 'ha', 'wa'), may hold values from -6 to 6
- output_cotangent: bfloat16 [32, 8, 16, 1536], P(None, 'ha', 'wa'), may hold values from -6 to 6
- window: int32 [12, 4], replicated, may hold values from 0 to 2, as said below
Outputs:
- attention_output: bfloat16 [32, 8, 16, 1536], P(None, 'ha', 'wa')
- key_gradient: bfloat16 [32, 8, 16, 1536], P(None, 'ha', 'wa')
- value_gradient: bfloat16 [32, 8, 16, 1536], P(None, 'ha', 'wa')
- weight_gradient: bfloat16 [1536, 1536], P('wa', 'ha')
The draws below stay inside these ranges and needn't reach their ends.
Inputs may be any that keep to these rules, and one draw needn't show every extreme that they name: `window`: row n is head n's (tile size s, reach in tiles along frames, reach in cells along rows, reach in cells along columns) with s one of 1, 2, the frame reach 0 to 2 and s times the frame reach at most 2, the row and column reaches 0 or 1; some head has s = 2 and reaches 1, 1, 1.
All inputs are finite; a program needn't handle non-finite values.
Results may differ from the reference program's by a relative error of at most 0.035.
Values may be sent and summed in bfloat16 or wider, within the bound.
A program may use at most 128 MiB of HBM per device.

```python
import math
import jax
import jax.numpy as jnp
from jax import lax

D = 1536
HEADS = 12
HD = 128
FRAMES = 32
HEIGHT = 8
BREADTH = 16
N_HA = 4
N_WA = 8


def query_key_pair(key):
    grid_shape = (FRAMES, HEIGHT, BREADTH, HEADS, HD)
    streams = jax.random.split(key, 2)
    queries = jax.random.normal(streams[0], grid_shape, jnp.float32)
    key_rows = jax.random.normal(streams[1], grid_shape, jnp.float32)
    queries = jnp.clip(queries, -256.0, 256.0)
    key_rows = jnp.clip(key_rows, -32.0, 32.0)
    flat_shape = (FRAMES, HEIGHT, BREADTH, HEADS * HD)
    return (queries.reshape(flat_shape), key_rows.reshape(flat_shape))


def draw_query_vectors(key, part):
    return query_key_pair(jax.random.fold_in(key, 5))[0].astype(jnp.bfloat16)


def draw_key_vectors(key, part):
    return query_key_pair(jax.random.fold_in(key, 5))[1].astype(jnp.bfloat16)


def draw_window(key, part):
    streams = jax.random.split(key, 5)
    tile_size = jax.random.randint(streams[0], (HEADS,), 1, 3).astype(jnp.int32)
    frame_reach = jax.random.randint(streams[1], (HEADS,), 0, 3).astype(jnp.int32)
    frame_reach = jnp.where(tile_size == 2, frame_reach % 2, frame_reach)
    row_reach = jax.random.randint(streams[2], (HEADS,), 0, 2)
    column_reach = jax.random.randint(streams[3], (HEADS,), 0, 2)
    order = jax.random.permutation(streams[4], HEADS)
    head_ids = jnp.arange(HEADS, dtype=jnp.int32)
    widest = head_ids == order[0]
    narrowest = head_ids == order[1]
    tile_size = jnp.where(widest, 2, jnp.where(narrowest, 1, tile_size))
    frame_reach = jnp.where(widest, 1, jnp.where(narrowest, 0, frame_reach))
    row_reach = jnp.where(widest, 1, jnp.where(narrowest, 0, row_reach))
    column_reach = jnp.where(widest, 1, jnp.where(narrowest, 0, column_reach))
    return jnp.stack([tile_size, frame_reach, row_reach, column_reach], axis=1).astype(jnp.int32)


def with_spikes(array, rng, source, target, blocks, factor):
    def block_of(axis_at):
        return (jnp.arange(array.shape[axis_at]) // (array.shape[axis_at] // blocks)).reshape((-1,) + (1,) * (array.ndim - 1 - axis_at))

    near = jax.random.permutation(rng, blocks)[block_of(target)]
    other_side = (block_of(target) + blocks // 2) % blocks
    return jnp.where((block_of(source) == near) | (block_of(source) == other_side), factor * array, array)


def levels(stream_key, shape, cuts, smallest, high):
    gain = 1.0
    for axis_at, shards_of in cuts:
        heights = jax.random.uniform(jax.random.fold_in(jax.random.fold_in(stream_key, 6), axis_at), (shards_of,), jnp.float32, smallest / len(cuts), high / len(cuts))
        gain = gain * jnp.repeat(jnp.exp(heights), shape[axis_at] // shards_of).reshape((-1,) + (1,) * (len(shape) - 1 - axis_at))
    return gain


def bell_draw(stream_key, extent, width, most, pieces=(), kind=jnp.bfloat16):
    loudness = levels(stream_key, extent, pieces, -0.22, 0.18) if pieces else 1.0
    entries = jax.random.normal(stream_key, extent, jnp.float32) * width * loudness
    return jnp.minimum(jnp.maximum(entries, -most), most).astype(kind)


def noise_with(stream_key, extent, width, limit, pieces, heavy, kind=jnp.bfloat16):
    drawn = width * jax.random.normal(stream_key, extent, jnp.float32)
    if pieces:
        drawn = drawn * levels(stream_key, extent, pieces, -0.22, 0.18)
    return jnp.clip(with_spikes(drawn, jax.random.fold_in(stream_key, 3), *heavy), -limit, limit).astype(kind)


def setup_inputs(seed: int = 0) -> dict:
    streams_of = jax.random.split(jax.random.key(seed), 7)
    return {
        "inputs": noise_with(streams_of[0], (FRAMES, HEIGHT, BREADTH, D), 1.0, 6.0, ((1, 4), (2, 8)), (2, 3, 8, 2.0)),
        "query_vectors": draw_query_vectors(jax.random.fold_in(streams_of[6], 71), 0),
        "key_vectors": draw_key_vectors(jax.random.fold_in(streams_of[6], 71), 0),
        "value_vectors": bell_draw(streams_of[3], (FRAMES, HEIGHT, BREADTH, HEADS * HD), 1.0, 6.0, ((1, 4), (2, 8))),
        "output_cotangent": bell_draw(streams_of[4], (FRAMES, HEIGHT, BREADTH, HEADS * HD), 1.0, 6.0, ((1, 4), (2, 8))),
        "window": draw_window(jax.random.fold_in(streams_of[6], 71), 0),
    }


def rounded(source):
    return lax.optimization_barrier(source.astype(jnp.bfloat16)).astype(jnp.float32)

def cell_grid(frames, span_rows, span_columns, row_start, column_start):
    grid_shape = (frames, span_rows, span_columns)
    frame_ids = lax.broadcasted_iota(jnp.int32, grid_shape, 0).reshape(-1)
    row_ids = (lax.broadcasted_iota(jnp.int32, grid_shape, 1) + row_start).reshape(-1)
    column_ids = (lax.broadcasted_iota(jnp.int32, grid_shape, 2) + column_start).reshape(-1)
    return (frame_ids, row_ids, column_ids)

def inside_grid(cells, height, breadth):
    return (cells[1] >= 0) & (cells[1] < height) & (cells[2] >= 0) & (cells[2] < breadth)

def visible(window, query_cells, key_cells, query_inside, key_inside):
    tile_size = window[:, 0][:, None, None]
    near_frame = jnp.abs(query_cells[0][None, :, None] // tile_size - key_cells[0][None, None, :] // tile_size) <= window[:, 1][:, None, None]
    near_row = jnp.abs(query_cells[1][None, :, None] - key_cells[1][None, None, :]) <= window[:, 2][:, None, None]
    near_column = jnp.abs(query_cells[2][None, :, None] - key_cells[2][None, None, :]) <= window[:, 3][:, None, None]
    both_inside = (query_inside[:, None] & key_inside[None, :])[None]
    return near_frame & near_row & near_column & both_inside

def reference(inputs, query_vectors, key_vectors, value_vectors, output_cotangent, window):
    frames, height, breadth, feature = query_vectors.shape
    head_count = window.shape[0]
    head_size = feature // head_count
    score_scale = 1.0 / math.sqrt(head_size)
    tile_rows = height // N_HA
    tile_columns = breadth // N_WA
    padded_rows = tile_rows + 2
    padded_columns = tile_columns + 2
    margin = ((0, 0), (1, 1), (1, 1), (0, 0))
    keys_padded = jnp.pad(key_vectors, margin)
    values_padded = jnp.pad(value_vectors, margin)
    blocks = jnp.arange(N_HA * N_WA, dtype=jnp.int32)
    anchor = jnp.zeros((), jnp.int32)

    def cut_slab(source, row_start, column_start, span_rows, span_columns):
        return lax.dynamic_slice(source, (anchor, row_start, column_start, anchor), (frames, span_rows, span_columns, source.shape[3]))

    def split_heads(source):
        return source.reshape(-1, head_count, head_size).astype(jnp.float32)

    def forward_step(weight_sum, block_index):
        row_start = block_index // N_WA * tile_rows
        column_start = block_index % N_WA * tile_columns
        query_heads = split_heads(cut_slab(query_vectors, row_start, column_start, tile_rows, tile_columns))
        key_padded = split_heads(cut_slab(keys_padded, row_start, column_start, padded_rows, padded_columns))
        value_padded = split_heads(cut_slab(values_padded, row_start, column_start, padded_rows, padded_columns))
        cotangent = split_heads(cut_slab(output_cotangent, row_start, column_start, tile_rows, tile_columns))
        token_rows = cut_slab(inputs, row_start, column_start, tile_rows, tile_columns).reshape(-1, inputs.shape[3])
        query_cells = cell_grid(frames, tile_rows, tile_columns, row_start, column_start)
        key_cells = cell_grid(frames, padded_rows, padded_columns, row_start - 1, column_start - 1)
        allowed = visible(window, query_cells, key_cells, query_cells[0] >= 0, inside_grid(key_cells, height, breadth))
        scores = jnp.where(allowed, jnp.einsum('qhd,khd->hqk', query_heads, key_padded) * score_scale, -jnp.inf)
        row_max = lax.optimization_barrier(jnp.max(scores, axis=2, keepdims=True))
        log_total = row_max + jnp.log(lax.optimization_barrier(jnp.sum(jnp.exp(scores - row_max), axis=2, keepdims=True)))
        probability = rounded(jnp.exp(scores - log_total))
        attended = rounded(jnp.einsum('hqk,khd->qhd', probability, value_padded))
        delta_rows = jnp.einsum('qhd,qhd->hq', cotangent, attended)
        upstream = jnp.einsum('qhd,khd->hqk', cotangent, value_padded)
        score_slopes = rounded(probability * (upstream - delta_rows[:, :, None]))
        query_slopes = (jnp.einsum('hqk,khd->qhd', score_slopes, key_padded) * score_scale).astype(jnp.bfloat16)
        block_term = jnp.dot(token_rows.T, query_slopes.reshape(-1, feature), preferred_element_type=jnp.float32)
        weight_sum = weight_sum + rounded(block_term)
        outputs = (attended.astype(jnp.bfloat16).reshape(frames, tile_rows, tile_columns, feature), log_total[:, :, 0], delta_rows)
        return (weight_sum, outputs)
    initial = jnp.zeros((inputs.shape[3], feature), jnp.float32)
    weight_sum, (attended_blocks, log_blocks, delta_blocks) = lax.scan(forward_step, initial, blocks)

    def as_grid(per_block):
        arranged = per_block.reshape(N_HA, N_WA, frames, tile_rows, tile_columns, -1)
        return arranged.transpose(2, 0, 3, 1, 4, 5).reshape(frames, height, breadth, -1)

    def stats_grid(per_block):
        return as_grid(per_block.transpose(0, 2, 1).reshape(N_HA * N_WA, frames, tile_rows, tile_columns, head_count))
    attention_output = as_grid(attended_blocks)
    log_padded = jnp.pad(stats_grid(log_blocks), margin)
    delta_padded = jnp.pad(stats_grid(delta_blocks), margin)
    queries_padded = jnp.pad(query_vectors, margin)
    cotangent_padded = jnp.pad(output_cotangent, margin)
    row_ranges = ((0, 1), (1, tile_rows + 1), (tile_rows + 1, padded_rows))
    column_ranges = ((0, 1), (1, tile_columns + 1), (tile_columns + 1, padded_columns))

    def key_step(block_index):
        row_start = block_index // N_WA * tile_rows
        column_start = block_index % N_WA * tile_columns
        key_block = split_heads(cut_slab(key_vectors, row_start, column_start, tile_rows, tile_columns))
        value_block = split_heads(cut_slab(value_vectors, row_start, column_start, tile_rows, tile_columns))
        key_cells = cell_grid(frames, tile_rows, tile_columns, row_start, column_start)
        key_inside = key_cells[0] >= 0
        key_total = jnp.zeros(key_block.shape, jnp.float32)
        value_total = jnp.zeros(key_block.shape, jnp.float32)
        for row_low, row_high in row_ranges:
            for column_low, column_high in column_ranges:
                span_rows = row_high - row_low
                span_columns = column_high - column_low
                query_heads = split_heads(cut_slab(queries_padded, row_start + row_low, column_start + column_low, span_rows, span_columns))
                cotangent = split_heads(cut_slab(cotangent_padded, row_start + row_low, column_start + column_low, span_rows, span_columns))
                log_part = cut_slab(log_padded, row_start + row_low, column_start + column_low, span_rows, span_columns).reshape(-1, head_count).T
                delta_part = cut_slab(delta_padded, row_start + row_low, column_start + column_low, span_rows, span_columns).reshape(-1, head_count).T
                query_cells = cell_grid(frames, span_rows, span_columns, row_start + row_low - 1, column_start + column_low - 1)
                allowed = visible(window, query_cells, key_cells, inside_grid(query_cells, height, breadth), key_inside)
                scores = jnp.where(allowed, jnp.einsum('qhd,khd->hqk', query_heads, key_block) * score_scale, -jnp.inf)
                probability = rounded(jnp.exp(scores - log_part[:, :, None]))
                value_part = jnp.einsum('hqk,qhd->khd', probability, cotangent)
                upstream = jnp.einsum('qhd,khd->hqk', cotangent, value_block)
                score_slopes = rounded(probability * (upstream - delta_part[:, :, None]))
                key_part = jnp.einsum('hqk,qhd->khd', score_slopes, query_heads) * score_scale
                if row_low == 1 and column_low == 1:
                    key_total = key_total + key_part
                    value_total = value_total + value_part
                else:
                    key_total = key_total + rounded(key_part)
                    value_total = value_total + rounded(value_part)
        key_out = key_total.astype(jnp.bfloat16).reshape(frames, tile_rows, tile_columns, feature)
        value_out = value_total.astype(jnp.bfloat16).reshape(frames, tile_rows, tile_columns, feature)
        return (key_out, value_out)
    key_blocks, value_blocks = lax.map(key_step, blocks)
    key_gradient = as_grid(key_blocks)
    value_gradient = as_grid(value_blocks)
    weight_gradient = (weight_sum * (1.0 / math.sqrt(frames * height * breadth))).astype(jnp.bfloat16)
    return (attention_output, key_gradient, value_gradient, weight_gradient)
```

```python
import functools
import math

import jax
import jax.numpy as jnp
from jax import lax
from jax.experimental import pallas as pl
from jax.experimental.pallas import tpu as pltpu
from jax.sharding import PartitionSpec as P

MESH = pl.DeviceIdType.MESH
GROUPS = 4


def attention_kernel(
    groups,
    window_hbm,
    q_ref,
    do_ref,
    own_ref,
    x_ref,
    att_ref,
    grad_ref,
    weight_ref,
    window_ref,
    padded,
    terms,
    from_side,
    from_row,
    slopes_own,
    x_all,
    slopes_all,
    product,
    from_partner,
    pair_sums,
    from_chips,
    local_sem,
    send_sem,
    recv_sem,
    x_send,
    x_recv,
    forward_send,
    forward_recv,
    slope_send,
    slope_recv,
    pair_send,
    pair_recv,
    chip_send,
    chip_recv,
):
    head_count, _, rows, columns, frames, head_size = own_ref.shape
    per_group = head_count // groups
    scale = 1.0 / math.sqrt(head_size)
    ha_count, wa_count = lax.axis_size("ha"), lax.axis_size("wa")
    ha, wa = lax.axis_index("ha"), lax.axis_index("wa")
    exists = {
        ("ha", -1): ha > 0,
        ("ha", 1): ha < ha_count - 1,
        ("wa", -1): wa > 0,
        ("wa", 1): wa < wa_count - 1,
    }
    place = {"ha": ha, "wa": wa}

    center = pltpu.make_async_copy(
        own_ref, padded.at[:, :, pl.ds(1, rows), pl.ds(1, columns)], local_sem.at[0]
    )
    center.start()
    unit = slopes_own.shape[2]
    share = slopes_all.shape[1]
    core, chip = wa % 2, wa // 2
    chips = wa_count // 2
    own_x = pltpu.make_async_copy(x_ref, x_all.at[ha], local_sem.at[1])
    own_x.start()
    window_copy = pltpu.make_async_copy(window_hbm, window_ref, local_sem.at[2])
    window_copy.start()

    @pl.when(ha == 0)
    def _():
        padded[:, :, 0] = jnp.zeros(padded.shape[:2] + padded.shape[3:], padded.dtype)
        from_row[0] = jnp.zeros(from_row.shape[1:], from_row.dtype)

    @pl.when(ha == ha_count - 1)
    def _():
        padded[:, :, rows + 1] = jnp.zeros(padded.shape[:2] + padded.shape[3:], padded.dtype)
        from_row[1] = jnp.zeros(from_row.shape[1:], from_row.dtype)

    @pl.when(wa == 0)
    def _():
        padded[:, :, :, 0] = jnp.zeros(padded.shape[:3] + padded.shape[4:], padded.dtype)
        from_side[0] = jnp.zeros(from_side.shape[1:], from_side.dtype)

    @pl.when(wa == wa_count - 1)
    def _():
        padded[:, :, :, columns + 1] = jnp.zeros(
            padded.shape[:3] + padded.shape[4:], padded.dtype
        )
        from_side[1] = jnp.zeros(from_side.shape[1:], from_side.dtype)

    barrier = pltpu.get_barrier_semaphore()
    for axis, count in (("ha", ha_count), ("wa", wa_count)):
        for step in range(1, count):
            pl.semaphore_signal(
                barrier,
                inc=1,
                device_id={axis: (place[axis] + step) % count},
                device_id_type=MESH,
            )
    pl.semaphore_wait(barrier, ha_count + wa_count - 2)

    def copy_of(phase, by, group):
        heads = pl.ds(group * per_group, per_group)
        inner_columns = pl.ds(1, columns)
        low = by < 0
        if phase == 0:
            source = own_ref.at[heads, :, 0 if low else rows - 1]
            target = padded.at[heads, :, rows + 1 if low else 0, inner_columns]
        elif phase == 1:
            source = padded.at[heads, :, :, 1 if low else columns]
            target = padded.at[heads, :, :, columns + 1 if low else 0]
        elif phase == 2:
            source = terms.at[heads, :, :, 0 if low else columns + 1]
            target = from_side.at[1 if low else 0, heads]
        else:
            source = terms.at[heads, :, 0 if low else rows + 1, inner_columns]
            target = from_row.at[1 if low else 0, heads]
        axis = "ha" if phase in (0, 3) else "wa"
        side = 0 if low else 1
        return axis, pltpu.make_async_remote_copy(
            src_ref=source,
            dst_ref=target,
            send_sem=send_sem.at[phase, side, group],
            recv_sem=recv_sem.at[phase, side, group],
            device_id={axis: place[axis] + by},
            device_id_type=MESH,
        )

    def start(phase, group):
        for by in (-1, 1):
            axis, copy = copy_of(phase, by, group)

            @pl.when(exists[axis, by])
            def _():
                copy.start()

    def arrived(phase, group):
        for by in (-1, 1):
            axis, copy = copy_of(phase, by, group)

            @pl.when(exists[axis, -by])
            def _():
                copy.wait_recv()

    def sent(phase, group):
        for by in (-1, 1):
            axis, copy = copy_of(phase, by, group)

            @pl.when(exists[axis, by])
            def _():
                copy.wait_send()

    def x_copy(peer):
        return pltpu.make_async_remote_copy(
            src_ref=x_ref,
            dst_ref=x_all.at[ha],
            send_sem=x_send.at[peer],
            recv_sem=x_recv.at[ha],
            device_id={"ha": peer},
            device_id_type=MESH,
        )

    low, high = ha % 2, ha // 2
    partner = 2 * high + 1 - low
    pairs = ha_count // 2
    half = x_ref.shape[0] // 2

    def forward_copy(part, slot, peer, mark):
        tokens = pl.ds(part * half, half)
        return pltpu.make_async_remote_copy(
            src_ref=x_all.at[slot, tokens],
            dst_ref=x_all.at[slot, tokens],
            send_sem=forward_send.at[part, mark],
            recv_sem=forward_recv.at[part, slot],
            device_id={"ha": peer},
            device_id_type=MESH,
        )

    def slope_copy(peer):
        return pltpu.make_async_remote_copy(
            src_ref=slopes_own.at[pl.ds(peer * share, share)],
            dst_ref=slopes_all.at[ha],
            send_sem=slope_send.at[peer],
            recv_sem=slope_recv.at[ha],
            device_id={"ha": peer},
            device_id_type=MESH,
        )

    def chip_copy(peer):
        return pltpu.make_async_remote_copy(
            src_ref=pair_sums.at[peer],
            dst_ref=from_chips.at[chip],
            send_sem=chip_send.at[peer],
            recv_sem=chip_recv.at[chip],
            device_id={"wa": 2 * peer + core},
            device_id_type=MESH,
        )

    def pair_copy(step):
        return pltpu.make_async_remote_copy(
            src_ref=product.at[step, 1 - core],
            dst_ref=from_partner.at[step],
            send_sem=pair_send.at[step],
            recv_sem=pair_recv.at[step],
            device_id={"wa": wa + 1 - 2 * core},
            device_id_type=MESH,
        )

    def landed(buffer, sems, peer):
        pltpu.make_async_copy(buffer.at[peer], buffer.at[peer], sems.at[peer]).wait()

    for group in range(groups):
        start(0, group)
    x_copy(partner).start()
    for pair in range(pairs):

        @pl.when(pair != high)
        def _(pair=pair):
            x_copy(2 * pair + low).start()

    center.wait()
    window_copy.wait()

    queries = rows * columns * frames
    keys = (rows + 2) * (columns + 2) * frames
    query_id = lax.broadcasted_iota(jnp.int32, (queries, 1), 0)
    key_id = lax.broadcasted_iota(jnp.int32, (1, keys), 1)
    query_frame = query_id % frames
    query_row = query_id // (frames * columns)
    query_column = (query_id // frames) % columns
    key_frame = key_id % frames
    key_row = key_id // (frames * (columns + 2)) - 1
    key_column = (key_id // frames) % (columns + 2) - 1
    outside = (
        (key_row + ha * rows < 0)
        | (key_row + ha * rows >= ha_count * rows)
        | (key_column + wa * columns < 0)
        | (key_column + wa * columns >= wa_count * columns)
    )
    key_row = jnp.where(outside, 1000, key_row)
    row_gap = jnp.abs(query_row - key_row)
    column_gap = jnp.abs(query_column - key_column)

    def head_step(head, carry):
        tile = window_ref[head, 0]
        q = q_ref[head].reshape(queries, head_size)
        do = do_ref[head].reshape(queries, head_size)
        k = padded[head, 0].reshape(keys, head_size)
        v = padded[head, 1].reshape(keys, head_size)
        query_tile = jnp.where(tile == 2, query_frame >> 1, query_frame)
        key_tile = jnp.where(tile == 2, key_frame >> 1, key_frame)
        allowed = (
            (jnp.abs(query_tile - key_tile) <= window_ref[head, 1])
            & (row_gap <= window_ref[head, 2])
            & (column_gap <= window_ref[head, 3])
        )
        across = (((1,), (1,)), ((), ()))
        down = (((0,), (0,)), ((), ()))
        dot = functools.partial(lax.dot_general, preferred_element_type=jnp.float32)
        scores = jnp.where(allowed, dot(q, k, across) * scale, -jnp.inf)
        top = jnp.max(scores, axis=1, keepdims=True)
        lifted = jnp.exp(scores - top)
        total = jnp.sum(lifted, axis=1, keepdims=True)
        weight = (lifted * (1.0 / total)).astype(jnp.bfloat16)
        att = jnp.dot(weight, v, preferred_element_type=jnp.float32).astype(jnp.bfloat16)
        att_ref[head] = att.reshape(att_ref.shape[1:])
        delta = jnp.sum(
            do.astype(jnp.float32) * att.astype(jnp.float32), axis=1, keepdims=True
        )
        upstream = dot(do, v, across)
        slopes = (weight.astype(jnp.float32) * (upstream - delta)).astype(jnp.bfloat16)
        dq = jnp.dot(slopes, k, preferred_element_type=jnp.float32) * scale
        dq = dq.astype(jnp.bfloat16)
        pieces = head_size // unit
        for piece in range(pieces):
            slopes_own[head * pieces + piece] = dq[:, piece * unit : (piece + 1) * unit]
        dk = dot(slopes, q, down) * scale
        terms[head, 0] = dk.astype(jnp.bfloat16).reshape(terms.shape[2:])
        dv = dot(weight, do, down)
        terms[head, 1] = dv.astype(jnp.bfloat16).reshape(terms.shape[2:])
        return carry

    def pass_on(group):
        arrived(0, group)
        start(1, group)

    def fold_sides(group):
        heads = pl.ds(group * per_group, per_group)
        arrived(2, group)
        terms[heads, :, :, 1] = terms[heads, :, :, 1] + from_side[0, heads]
        terms[heads, :, :, columns] = terms[heads, :, :, columns] + from_side[1, heads]
        start(3, group)

    def fold_rows(group):
        heads = pl.ds(group * per_group, per_group)
        arrived(3, group)
        for row in range(rows):
            value = terms[heads, :, row + 1, pl.ds(1, columns)]
            if row == 0:
                value = value + from_row[0, heads]
            if row == rows - 1:
                value = value + from_row[1, heads]
            grad_ref[heads, :, row] = value

    pass_on(0)
    if groups > 1:
        pass_on(1)
    for group in range(groups):
        arrived(1, group)
        lax.fori_loop(group * per_group, (group + 1) * per_group, head_step, 0)
        start(2, group)
        for peer in range(ha_count):
            last = ((peer + 1) * share * unit - 1) // head_size
            if last // per_group == group:

                @pl.when(peer != ha)
                def _(peer=peer):
                    slope_copy(peer).start()

                @pl.when(peer == ha)
                def _(peer=peer):
                    slopes_all[peer] = slopes_own[pl.ds(peer * share, share)]

        if group + 2 < groups:
            pass_on(group + 2)

    landed(x_all, x_recv, partner)
    for pair in range(pairs):

        @pl.when(pair != high)
        def _(pair=pair):
            forward_copy(0, partner, 2 * pair + low, pair).start()

    for pair in range(pairs):

        @pl.when(pair != high)
        def _(pair=pair):
            landed(x_all, x_recv, 2 * pair + low)
            forward_copy(1, 2 * pair + low, partner, pair).start()

    for group in range(groups):
        fold_sides(group)

    own_x.wait()
    for peer in range(ha_count):

        @pl.when(peer != ha)
        def _(peer=peer):
            landed(slopes_all, slope_recv, peer)

    for pair in range(pairs):

        @pl.when(pair != high)
        def _(pair=pair):
            slot = 2 * pair + 1 - low
            for part in range(2):
                forward_copy(part, slot, partner, pair).wait_recv()

    block = x_all.shape[2] // chips

    for step in range(chips):
        total = jnp.zeros((block, share * unit), jnp.float32)
        for peer in range(ha_count):
            left = x_all[peer, :, step * block : (step + 1) * block]
            right = jnp.concatenate([slopes_all[peer, at] for at in range(share)], axis=1)
            total = total + lax.dot_general(
                left, right, (((0,), (0,)), ((), ())), preferred_element_type=jnp.float32
            )
        product[step] = total.astype(product.dtype).reshape(product.shape[1:])
        pair_copy(step).start()

    for peer in range(chips):
        pair_copy(peer).wait_recv()
        both = product[peer, core].astype(jnp.float32) + from_partner[peer].astype(jnp.float32)
        pair_sums[peer] = both.astype(pair_sums.dtype)

        @pl.when(peer != chip)
        def _(peer=peer):
            chip_copy(peer).start()

        @pl.when(peer == chip)
        def _(peer=peer):
            from_chips[peer] = pair_sums[peer]

    for group in range(groups):
        fold_rows(group)
    for peer in range(chips):

        @pl.when(peer != chip)
        def _(peer=peer):
            landed(from_chips, chip_recv, peer)

    gathered = from_chips[0].astype(jnp.float32)
    for peer in range(1, chips):
        gathered = gathered + from_chips[peer].astype(jnp.float32)
    tokens_all = queries * ha_count * wa_count
    weight_ref[...] = (gathered * (1.0 / math.sqrt(tokens_all))).astype(weight_ref.dtype)

    for phase in range(4):
        for group in range(groups):
            sent(phase, group)
    for peer in range(ha_count):

        @pl.when(peer != ha)
        def _(peer=peer):
            slope_copy(peer).wait_send()

    x_copy(partner).wait_send()
    for pair in range(pairs):

        @pl.when(pair != high)
        def _(pair=pair):
            x_copy(2 * pair + low).wait_send()
            forward_copy(0, partner, 2 * pair + low, pair).wait_send()
            forward_copy(1, 2 * pair + low, partner, pair).wait_send()

    for peer in range(chips):
        pair_copy(peer).wait_send()

        @pl.when(peer != chip)
        def _(peer=peer):
            chip_copy(peer).wait_send()


def on_device(branch, inputs, query_vectors, key_vectors, value_vectors, output_cotangent, window):
    frames, rows, columns, feature = query_vectors.shape
    head_count = window.shape[0]
    head_size = feature // head_count
    queries = frames * rows * columns
    groups = math.gcd(GROUPS, head_count)

    def by_head(x):
        return x.reshape(frames, rows, columns, head_count, head_size).transpose(3, 1, 2, 0, 4)

    q = by_head(query_vectors)
    do = by_head(output_cotangent)
    own = jnp.stack([by_head(key_vectors), by_head(value_vectors)], axis=1)
    bf = jnp.bfloat16
    flat_inputs = inputs.transpose(1, 2, 0, 3).reshape(queries, inputs.shape[3])
    ha_count, wa_count = lax.axis_size("ha"), lax.axis_size("wa")
    chips = wa_count // 2
    slice_rows = inputs.shape[3] // wa_count
    slice_columns = feature // ha_count
    unit = math.gcd(head_size, slice_columns)
    tall = (head_count, 2, rows + 2, columns + 2, frames, head_size)
    vmem = pl.BlockSpec(memory_space=pltpu.VMEM)
    att, grads, weight_gradient = pl.pallas_call(
        functools.partial(attention_kernel, groups),
        out_shape=(
            jax.ShapeDtypeStruct((head_count, rows, columns, frames, head_size), bf),
            jax.ShapeDtypeStruct((head_count, 2, rows, columns, frames, head_size), bf),
            jax.ShapeDtypeStruct((slice_rows, slice_columns), bf),
        ),
        in_specs=[pl.BlockSpec(memory_space=pl.ANY), vmem, vmem, vmem, vmem],
        out_specs=(vmem, vmem, vmem),
        scratch_shapes=[
            pltpu.SMEM(window.shape, window.dtype),
            pltpu.VMEM(tall, bf),
            pltpu.VMEM(tall, bf),
            pltpu.VMEM((2, head_count, 2, rows + 2, frames, head_size), bf),
            pltpu.VMEM((2, head_count, 2, columns, frames, head_size), bf),
            pltpu.VMEM((feature // unit, queries, unit), bf),
            pltpu.VMEM((ha_count, queries, inputs.shape[3]), bf),
            pltpu.VMEM((ha_count, slice_columns // unit, queries, unit), bf),
            pltpu.VMEM((chips, 2, slice_rows, slice_columns), bf),
            pltpu.VMEM((chips, slice_rows, slice_columns), bf),
            pltpu.VMEM((chips, slice_rows, slice_columns), bf),
            pltpu.VMEM((chips, slice_rows, slice_columns), bf),
            pltpu.SemaphoreType.DMA((3,)),
            pltpu.SemaphoreType.DMA((4, 2, groups)),
            pltpu.SemaphoreType.DMA((4, 2, groups)),
            pltpu.SemaphoreType.DMA((ha_count,)),
            pltpu.SemaphoreType.DMA((ha_count,)),
            pltpu.SemaphoreType.DMA((2, ha_count // 2)),
            pltpu.SemaphoreType.DMA((2, ha_count)),
            pltpu.SemaphoreType.DMA((ha_count,)),
            pltpu.SemaphoreType.DMA((ha_count,)),
            pltpu.SemaphoreType.DMA((chips,)),
            pltpu.SemaphoreType.DMA((chips,)),
            pltpu.SemaphoreType.DMA((chips,)),
            pltpu.SemaphoreType.DMA((chips,)),
        ],
        compiler_params=pltpu.CompilerParams(
            collective_id=branch, has_side_effects=True, vmem_limit_bytes=56 * 1024 * 1024
        ),
    )(window, q, do, own, flat_inputs)

    def to_grid(x):
        return x.transpose(3, 1, 2, 0, 4).reshape(frames, rows, columns, feature)

    attention_output = to_grid(att)
    key_gradient = to_grid(grads[:, 0])
    value_gradient = to_grid(grads[:, 1])
    return (attention_output, key_gradient, value_gradient, weight_gradient)


def by_reach(*args):
    many = jnp.sum(args[5][:, 2]) > 6
    return lax.cond(many, functools.partial(on_device, 1), functools.partial(on_device, 0), *args)


def solution(mesh):
    cells = P(None, "ha", "wa", None)
    return jax.shard_map(
        by_reach,
        mesh=mesh,
        in_specs=(cells, cells, cells, cells, cells, P()),
        out_specs=(cells, cells, cells, P("wa", "ha")),
        check_vma=False,
    )
```

```python
import functools
import math

import jax
import jax.numpy as jnp
from jax import lax
from jax.experimental import pallas as pl
from jax.experimental.pallas import tpu as pltpu
from jax.sharding import PartitionSpec as P

MESH = pl.DeviceIdType.MESH
TALLS = (4, 6, 8, 12)
BATCH = 3
CHUNKS = 4
HIDDEN = -1e30
FRAME_KINDS = ((1, 0), (1, 1), (1, 2), (2, 0), (2, 1))


def split(low, high):
    count = high - low
    runs = -(-count // BATCH)
    out = []
    for at in range(runs):
        size = count // runs + (1 if at < count % runs else 0)
        out.append((low, size))
        low += size
    return out


def attention_kernel(
    tall_count,
    window_ref,
    q_ref,
    do_ref,
    k_ref,
    v_ref,
    x_ref,
    att_ref,
    dk_ref,
    dv_ref,
    weight_ref,
    order_ref,
    pos_ref,
    kind_ref,
    code_ref,
    heads_kv,
    heads_q,
    heads_do,
    padded,
    terms,
    att_slots,
    dq_slots,
    from_side,
    from_row,
    relay_rows,
    relay_terms,
    slopes_own,
    x_all,
    slopes_all,
    product,
    from_partner,
    pair_sums,
    from_pair,
    chip_sums,
    from_chips,
    own_x_sem,
    row_send,
    row_recv,
    relay_send,
    relay_recv,
    col_send,
    col_recv,
    corner_send,
    corner_recv,
    side_send,
    side_recv,
    x_send,
    x_recv,
    forward_send,
    slope_send,
    slope_recv,
    core_send,
    core_recv,
    pair_send,
    pair_recv,
    chip_send,
    chip_recv,
):
    rows, columns, frames, _ = k_ref.shape
    head_count = padded.shape[0]
    head_size = padded.shape[-1]
    queries = q_ref.shape[0]
    bf = jnp.bfloat16
    scale = 1.0 / math.sqrt(head_size)
    ha_count, wa_count = lax.axis_size("ha"), lax.axis_size("wa")
    ha, wa = lax.axis_index("ha"), lax.axis_index("wa")
    flat_count = head_count - tall_count
    flat_runs = split(0, flat_count)
    tall_runs = split(flat_count, head_count)
    runs = flat_runs + tall_runs
    place = {"ha": ha, "wa": wa}
    exists = {
        ("ha", -1): ha > 0,
        ("ha", 1): ha < ha_count - 1,
        ("wa", -1): wa > 0,
        ("wa", 1): wa < wa_count - 1,
    }
    above, below = rows, rows + 1
    left, right = columns, columns + 1
    low, high = ha % 2, ha // 2
    partner = 2 * high + 1 - low
    pairs = ha_count // 2
    relayed = pairs == 2

    tall_slots = pl.ds(flat_count, tall_count)
    for at, side, line in ((0, 0, above), (ha_count - 1, 1, below)):

        @pl.when(ha == at)
        def _(side=side, line=line):
            hidden = padded.at[tall_slots, :, line]
            hidden[...] = jnp.zeros(hidden.shape, bf)
            from_row[side] = jnp.zeros(from_row.shape[1:], bf)

    for at, side, line in ((0, 0, left), (wa_count - 1, 1, right)):

        @pl.when(wa == at)
        def _(side=side, line=line):
            for count, first, lines in (
                (flat_count, 0, rows),
                (tall_count, flat_count, rows + 2),
            ):
                if count:
                    hidden = padded.at[pl.ds(first, count), :, pl.ds(0, lines), line]
                    hidden[...] = jnp.zeros(hidden.shape, bf)
                    fold = from_side.at[side, pl.ds(first, count), :, pl.ds(0, lines)]
                    fold[...] = jnp.zeros(fold.shape, bf)

    barrier = pltpu.get_barrier_semaphore()
    for axis, count in (("ha", ha_count), ("wa", wa_count)):
        for step in range(1, count):
            pl.semaphore_signal(
                barrier,
                inc=1,
                device_id={axis: (place[axis] + step) % count},
                device_id_type=MESH,
            )
    own_x = pltpu.make_async_copy(x_ref, x_all.at[ha], own_x_sem.at[0])
    own_x.start()

    reach = [window_ref[2, head] for head in range(head_count)]
    next_tall = head_count - sum(reach)
    next_flat = 0
    spots = []
    for head in range(head_count):
        spot = jnp.where(reach[head] > 0, next_tall, next_flat)
        next_tall = next_tall + reach[head]
        next_flat = next_flat + 1 - reach[head]
        pos_ref[head] = spot
        spots.append(spot)
    kinds = []
    for head in range(head_count):
        tile = jnp.where(window_ref[0, head] == 2, 3, 0) + window_ref[1, head]
        kinds.append(4 * tile + 2 * reach[head] + window_ref[3, head])
    for slot in range(head_count):
        here = [spots[head] == slot for head in range(head_count)]
        order_ref[slot] = sum(jnp.where(here[head], head, 0) for head in range(head_count))
        kind_ref[slot] = sum(jnp.where(here[head], kinds[head], 0) for head in range(head_count))

    for head in range(head_count):
        lanes = slice(head * head_size, (head + 1) * head_size)
        heads_kv[head, 0] = k_ref[:, :, :, lanes]
        heads_kv[head, 1] = v_ref[:, :, :, lanes]
    for slot in range(head_count):
        padded[slot, :, :rows, :columns] = heads_kv[order_ref[slot]]

    pl.semaphore_wait(barrier, ha_count + wa_count - 2)

    def remote(source, target, send, recv, axis, device):
        return pltpu.make_async_remote_copy(
            src_ref=source,
            dst_ref=target,
            send_sem=send,
            recv_sem=recv,
            device_id={axis: device},
            device_id_type=MESH,
        )

    def landed(buffer, sem):
        pltpu.make_async_copy(buffer, buffer, sem).wait()

    def detour(by):
        if not relayed:
            return None
        return ha == (1 if by > 0 else pairs)

    def row_source(kind, by, part, run):
        first, size = tall_runs[run]
        if kind == 0:
            return padded.at[
                pl.ds(first, size), part, 0 if by < 0 else rows - 1, pl.ds(0, columns)
            ]
        return terms.at[
            pl.ds(first, size), part, above if by < 0 else below, pl.ds(0, columns)
        ]

    def row_target(kind, by, part, run):
        first, size = tall_runs[run]
        if kind == 0:
            return padded.at[
                pl.ds(first, size), part, below if by < 0 else above, pl.ds(0, columns)
            ]
        return from_row.at[1 if by < 0 else 0, pl.ds(first - flat_count, size), part]

    def relay_buffer(kind, run):
        first, size = tall_runs[run]
        return (relay_rows, relay_terms)[kind].at[pl.ds(first - flat_count, size)]

    def row_copy(kind, by, part, run):
        side = 0 if by < 0 else 1
        return remote(
            row_source(kind, by, part, run),
            row_target(kind, by, part, run),
            row_send.at[kind, side, part, run],
            row_recv.at[kind, side, part, run],
            "ha",
            ha + by,
        )

    def detour_copy(kind, by, run):
        side = 0 if by < 0 else 1
        return remote(
            row_source(kind, by, 1, run),
            relay_buffer(kind, run),
            row_send.at[kind, side, 1, run],
            relay_recv.at[kind, run],
            "ha",
            (ha + 2) % ha_count,
        )

    def relay_copy(kind, by, run):
        side = 0 if by < 0 else 1
        return remote(
            relay_buffer(kind, run),
            row_target(kind, by, 1, run),
            relay_send.at[kind, run],
            row_recv.at[kind, side, 1, run],
            "ha",
            partner,
        )

    def each_row_copy(kind, run, act):
        for by in (-1, 1):
            turn = detour(by)
            for part in range(2):
                direct = exists["ha", by]
                if part == 1 and turn is not None:
                    direct = direct & jnp.logical_not(turn)

                    @pl.when(turn)
                    def _(by=by):
                        act(detour_copy(kind, by, run))

                @pl.when(direct)
                def _(by=by, part=part):
                    act(row_copy(kind, by, part, run))

    def start_rows(kind, run):
        each_row_copy(kind, run, lambda copy: copy.start())

    def relay(kind, run):
        if relayed:
            for at, by in ((0, -1), (ha_count - 1, 1)):

                @pl.when(ha == at)
                def _(by=by):
                    landed(relay_buffer(kind, run), relay_recv.at[kind, run])
                    relay_copy(kind, by, run).start()

    def rows_arrived(kind, run):
        for by in (-1, 1):

            @pl.when(exists["ha", -by])
            def _(by=by):
                for part in range(2):
                    row_copy(kind, by, part, run).wait_recv()

    def column_copy(kind, by, run):
        first, size = (tall_runs if kind == 1 else runs)[run]
        slots = pl.ds(first, size)
        side = 0 if by < 0 else 1
        if kind == 2:
            lines = pl.ds(0, rows if first < flat_count else rows + 2)
            source = terms.at[slots, :, lines, left if by < 0 else right]
            target = from_side.at[1 if by < 0 else 0, slots, :, lines]
        else:
            lines = pl.ds(0, rows) if kind == 0 else pl.ds(rows, 2)
            source = padded.at[slots, :, lines, 0 if by < 0 else columns - 1]
            target = padded.at[slots, :, lines, right if by < 0 else left]
        send = (col_send, corner_send, side_send)[kind]
        recv = (col_recv, corner_recv, side_recv)[kind]
        return remote(source, target, send.at[side, run], recv.at[side, run], "wa", wa + by)

    def start_columns(kind, run):
        for by in (-1, 1):

            @pl.when(exists["wa", by])
            def _(by=by):
                column_copy(kind, by, run).start()

    def columns_arrived(kind, run):
        for by in (-1, 1):

            @pl.when(exists["wa", -by])
            def _(by=by):
                column_copy(kind, by, run).wait_recv()

    chunk = queries // CHUNKS

    def x_copy(peer, part):
        tokens = pl.ds(part * chunk, chunk)
        return remote(
            x_ref.at[tokens],
            x_all.at[ha, tokens],
            x_send.at[peer, part],
            x_recv.at[ha, part],
            "ha",
            peer,
        )

    def forward_copy(pair, part):
        tokens = pl.ds(part * chunk, chunk)
        return remote(
            x_all.at[partner, tokens],
            x_all.at[partner, tokens],
            forward_send.at[pair, part],
            x_recv.at[partner, part],
            "ha",
            2 * pair + low,
        )

    def x_landed(peer, part):
        tokens = pl.ds(part * chunk, chunk)
        landed(x_all.at[peer, tokens], x_recv.at[peer, part])

    def other_pairs(act):
        for pair in range(pairs):

            @pl.when(pair != high)
            def _(pair=pair):
                act(pair)

    for run in range(len(tall_runs)):
        start_rows(0, run)
    for run in range(len(runs)):
        start_columns(0, run)
    for part in range(CHUNKS):
        x_copy(partner, part).start()
        other_pairs(lambda pair: x_copy(2 * pair + low, part).start())

    query_id = lax.broadcasted_iota(jnp.int32, (1, queries), 1)
    key_id = lax.broadcasted_iota(jnp.int32, (code_ref.shape[0], 1), 0)
    query_frame = query_id // (rows * columns)
    query_row = (query_id // columns) % rows
    query_column = query_id % columns
    key_frame = key_id % frames
    key_row = key_id // (frames * (columns + 2))
    key_column = (key_id // frames) % (columns + 2)
    key_row = jnp.where(key_row == above, -1, jnp.where(key_row == below, rows, key_row))
    key_column = jnp.where(
        key_column == left, -1, jnp.where(key_column == right, columns, key_column)
    )
    outside = (
        (key_row + ha * rows < 0)
        | (key_row + ha * rows >= ha_count * rows)
        | (key_column + wa * columns < 0)
        | (key_column + wa * columns >= wa_count * columns)
    )
    key_row = jnp.where(outside, 1000, key_row)
    row_gap = jnp.abs(query_row - key_row)
    column_gap = jnp.abs(query_column - key_column)
    cells = jnp.zeros(code_ref.shape, jnp.int32)
    for row_reach in range(2):
        for column_reach in range(2):
            near = (row_gap <= row_reach) & (column_gap <= column_reach)
            cells = cells | jnp.where(near, 1 << (2 * row_reach + column_reach), 0)
    code = jnp.zeros(code_ref.shape, jnp.int32)
    for kind, (tile, frame_reach) in enumerate(FRAME_KINDS):
        gap = jnp.abs(query_frame // tile - key_frame // tile)
        code = code | jnp.where(gap <= frame_reach, cells << (4 * kind), 0)
    code_ref[...] = code
    for head in range(head_count):
        lanes = slice(head * head_size, (head + 1) * head_size)
        heads_q[head] = q_ref[:, lanes]
        heads_do[head] = do_ref[:, lanes]

    across = (((1,), (1,)), ((), ()))
    down = (((0,), (0,)), ((), ()))
    dot = functools.partial(lax.dot_general, preferred_element_type=jnp.float32)
    lift = scale * math.log2(math.e)

    def attend(run):
        first, size = runs[run]
        lines = rows if first < flat_count else rows + 2
        keys = lines * (columns + 2) * frames
        slots = range(first, first + size)
        q = [heads_q[order_ref[slot]] for slot in slots]
        do = [heads_do[order_ref[slot]] for slot in slots]
        k = [padded[slot, 0, :lines].reshape(keys, head_size) for slot in slots]
        v = [padded[slot, 1, :lines].reshape(keys, head_size) for slot in slots]
        bits = [jnp.left_shift(1, kind_ref[slot]) for slot in slots]
        each = range(size)
        scores = [dot(k[i], q[i], across) for i in each]
        upstream = [dot(v[i], do[i], across) for i in each]
        scores = [
            jnp.where((code_ref[:keys] & bits[i]) != 0, scores[i], HIDDEN) for i in each
        ]
        top = [jnp.max(scores[i], axis=0, keepdims=True) for i in each]
        lifted = [jnp.exp2((scores[i] - top[i]) * lift) for i in each]
        total = [jnp.sum(lifted[i], axis=0, keepdims=True) for i in each]
        weight = [(lifted[i] * (1.0 / total[i])).astype(bf) for i in each]
        wide = [weight[i].astype(jnp.float32) for i in each]
        delta = [jnp.sum(wide[i] * upstream[i], axis=0, keepdims=True) for i in each]
        slopes = [(wide[i] * (upstream[i] - delta[i])).astype(bf) for i in each]
        shape = (lines,) + terms.shape[3:]
        for i, slot in enumerate(slots):
            dv = jnp.dot(weight[i], do[i], preferred_element_type=jnp.float32)
            terms[slot, 1, :lines] = dv.astype(bf).reshape(shape)
            dk = jnp.dot(slopes[i], q[i], preferred_element_type=jnp.float32) * scale
            terms[slot, 0, :lines] = dk.astype(bf).reshape(shape)
            att_slots[slot] = dot(weight[i], v[i], down).astype(bf)
            dq_slots[slot] = (dot(slopes[i], k[i], down) * scale).astype(bf)

    tall_base = len(flat_runs)
    opened = 0

    def open_tall(run):
        relay(0, run)
        rows_arrived(0, run)
        start_columns(1, run)

    for run in range(len(flat_runs)):
        columns_arrived(0, run)
        attend(run)
        start_columns(2, run)
        if opened < len(tall_runs):
            open_tall(opened)
            opened += 1
    for run in range(len(tall_runs)):
        while opened < min(run + 2, len(tall_runs)):
            open_tall(opened)
            opened += 1
        columns_arrived(0, tall_base + run)
        columns_arrived(1, run)
        attend(tall_base + run)
        start_columns(2, tall_base + run)

    unit = slopes_own.shape[2]
    share = slopes_all.shape[1]
    pieces = head_size // unit
    for head in range(head_count):
        value = dq_slots[pos_ref[head]]
        for piece in range(pieces):
            slopes_own[head * pieces + piece] = value[:, piece * unit : (piece + 1) * unit]

    def slope_copy(peer):
        return remote(
            slopes_own.at[pl.ds(peer * share, share)],
            slopes_all.at[ha],
            slope_send.at[peer],
            slope_recv.at[ha],
            "ha",
            peer,
        )

    for peer in range(ha_count):

        @pl.when(peer != ha)
        def _(peer=peer):
            slope_copy(peer).start()

        @pl.when(peer == ha)
        def _(peer=peer):
            slopes_all[peer] = slopes_own[pl.ds(peer * share, share)]

    for part in range(CHUNKS):
        x_landed(partner, part)
        other_pairs(lambda pair: forward_copy(pair, part).start())

    for head in range(head_count):
        att_ref[:, head * head_size : (head + 1) * head_size] = att_slots[pos_ref[head]]

    def fold_sides(run):
        first, size = runs[run]
        slots = pl.ds(first, size)
        lines = rows if first < flat_count else rows + 2
        columns_arrived(2, run)
        for side, line in ((0, 0), (1, columns - 1)):
            terms[slots, :, :lines, line] = (
                terms[slots, :, :lines, line] + from_side[side, slots, :, :lines]
            )

    for run in range(len(flat_runs)):
        fold_sides(run)

    own_x.wait()
    for peer in range(ha_count):

        @pl.when(peer != ha)
        def _(peer=peer):
            landed(slopes_all.at[peer], slope_recv.at[peer])

    def wait_others(pair):
        for part in range(CHUNKS):
            x_landed(2 * pair + low, part)
            x_landed(2 * pair + 1 - low, part)

    other_pairs(wait_others)

    core, chip = wa % 2, wa // 2
    chips = wa_count // 2
    halves = chips // 2
    parity, own_half = chip % 2, chip // 2
    block = x_all.shape[2] // chips
    tokens = ha_count * queries
    aligned = block % 128 == 0

    def core_copy(dest):
        return remote(
            product.at[dest, 1 - core],
            from_partner.at[dest],
            core_send.at[dest],
            core_recv.at[dest],
            "wa",
            wa + 1 - 2 * core,
        )

    def pair_copy(half):
        return remote(
            pair_sums.at[2 * half + 1 - parity],
            from_pair.at[half],
            pair_send.at[half],
            pair_recv.at[half],
            "wa",
            2 * (chip + 1 - 2 * parity) + core,
        )

    def chip_copy(half):
        return remote(
            chip_sums.at[half],
            from_chips.at[own_half],
            chip_send.at[half],
            chip_recv.at[own_half],
            "wa",
            2 * (2 * half + parity) + core,
        )

    stations = []
    for step in range(halves):
        half = lax.rem(own_half + 1 + step, halves)
        stations += [2 * half + 1 - parity, 2 * half + parity]
    columns_of = [slopes_all[:, at].reshape(tokens, unit) for at in range(share)]
    slope_block = columns_of[0] if share == 1 else jnp.concatenate(columns_of, axis=1)
    for step in range(chips):
        if aligned:
            dest = stations[step]
            token_block = x_all[:, :, pl.ds(pl.multiple_of(dest * block, block), block)]
        else:
            dest = step
            token_block = x_all[:, :, step * block : (step + 1) * block]
        value = dot(token_block.reshape(tokens, block), slope_block, down)
        product[dest] = value.astype(bf).reshape(product.shape[1:])
        core_copy(dest).start()

    for run in range(len(tall_runs)):
        fold_sides(tall_base + run)
        start_rows(1, run)

    for step in range(halves):
        half = lax.rem(own_half + 1 + step, halves)
        for dest in (2 * half + 1 - parity, 2 * half + parity):
            core_copy(dest).wait_recv()
            both = product[dest, core].astype(jnp.float32) + from_partner[dest].astype(
                jnp.float32
            )
            pair_sums[dest] = both.astype(bf)
        pair_copy(half).start()

    for run in range(len(tall_runs)):
        relay(1, run)

    for step in range(halves):
        half = lax.rem(own_half + 1 + step, halves)
        pair_copy(half).wait_recv()
        both = pair_sums[2 * half + parity].astype(jnp.float32) + from_pair[half].astype(
            jnp.float32
        )
        chip_sums[half] = both.astype(bf)
        if step < halves - 1:
            chip_copy(half).start()
        else:
            from_chips[half] = chip_sums[half]

    for run in range(len(tall_runs)):
        rows_arrived(1, run)
        first, size = tall_runs[run]
        slots = pl.ds(first, size)
        near = pl.ds(first - flat_count, size)
        for side, line in ((0, 0), (1, rows - 1)):
            terms[slots, :, line, :columns] = (
                terms[slots, :, line, :columns] + from_row[side, near]
            )

    for head in range(head_count):
        here = slice(head * head_size, (head + 1) * head_size)
        dk_ref[:, :, :, here] = terms[pos_ref[head], 0, :rows, :columns]
        dv_ref[:, :, :, here] = terms[pos_ref[head], 1, :rows, :columns]

    for step in range(halves - 1):
        half = lax.rem(own_half + 1 + step, halves)
        landed(from_chips.at[half], chip_recv.at[half])
    gathered = from_chips[0].astype(jnp.float32)
    for half in range(1, halves):
        gathered = gathered + from_chips[half].astype(jnp.float32)
    tokens_all = queries * ha_count * wa_count
    weight_ref[...] = (gathered * (1.0 / math.sqrt(tokens_all))).astype(weight_ref.dtype)

    for kind in range(2):
        for run in range(len(tall_runs)):
            each_row_copy(kind, run, lambda copy: copy.wait_send())
            if relayed:
                for at, by in ((0, -1), (ha_count - 1, 1)):

                    @pl.when(ha == at)
                    def _(by=by, kind=kind, run=run):
                        relay_copy(kind, by, run).wait_send()

    for kind, count in ((0, len(runs)), (1, len(tall_runs)), (2, len(runs))):
        for run in range(count):
            for by in (-1, 1):

                @pl.when(exists["wa", by])
                def _(by=by, kind=kind, run=run):
                    column_copy(kind, by, run).wait_send()

    def x_sent(pair):
        for part in range(CHUNKS):
            x_copy(2 * pair + low, part).wait_send()
            forward_copy(pair, part).wait_send()

    for part in range(CHUNKS):
        x_copy(partner, part).wait_send()
    other_pairs(x_sent)
    for peer in range(ha_count):

        @pl.when(peer != ha)
        def _(peer=peer):
            slope_copy(peer).wait_send()

    for dest in range(chips):
        core_copy(dest).wait_send()
    for half in range(halves):
        pair_copy(half).wait_send()
    for step in range(halves - 1):
        chip_copy(lax.rem(own_half + 1 + step, halves)).wait_send()


def on_device(
    which, inputs, query_vectors, key_vectors, value_vectors, output_cotangent, window
):
    tall_count = TALLS[which]
    frames, rows, columns, feature = query_vectors.shape
    head_count = window.shape[0]
    head_size = feature // head_count
    queries = frames * rows * columns
    bf = jnp.bfloat16

    def tokens(x):
        return x.reshape(queries, x.shape[3])

    def cells(x):
        return x.transpose(1, 2, 0, 3)

    ha_count, wa_count = lax.axis_size("ha"), lax.axis_size("wa")
    chips = wa_count // 2
    halves = chips // 2
    slice_rows = inputs.shape[3] // wa_count
    slice_columns = feature // ha_count
    unit = math.gcd(head_size, slice_columns)
    cell = (frames, head_size)
    tall = (head_count, 2, rows + 2, columns + 2) + cell
    keys = (rows + 2) * (columns + 2) * frames
    part = (slice_rows, slice_columns)
    tall_runs = len(split(head_count - tall_count, head_count))
    runs = len(split(0, head_count - tall_count)) + tall_runs
    vmem = pl.BlockSpec(memory_space=pltpu.VMEM)
    dma = pltpu.SemaphoreType.DMA
    att, dk, dv, weight_gradient = pl.pallas_call(
        functools.partial(attention_kernel, tall_count),
        out_shape=(
            jax.ShapeDtypeStruct((queries, feature), bf),
            jax.ShapeDtypeStruct((rows, columns, frames, feature), bf),
            jax.ShapeDtypeStruct((rows, columns, frames, feature), bf),
            jax.ShapeDtypeStruct(part, bf),
        ),
        in_specs=[pl.BlockSpec(memory_space=pltpu.SMEM), vmem, vmem, vmem, vmem, vmem],
        out_specs=(vmem, vmem, vmem, vmem),
        scratch_shapes=[
            pltpu.SMEM((head_count,), jnp.int32),
            pltpu.SMEM((head_count,), jnp.int32),
            pltpu.SMEM((head_count,), jnp.int32),
            pltpu.VMEM((keys, queries), jnp.int32),
            pltpu.VMEM((head_count, 2, rows, columns) + cell, bf),
            pltpu.VMEM((head_count, queries, head_size), bf),
            pltpu.VMEM((head_count, queries, head_size), bf),
            pltpu.VMEM(tall, bf),
            pltpu.VMEM(tall, bf),
            pltpu.VMEM((head_count, queries, head_size), bf),
            pltpu.VMEM((head_count, queries, head_size), bf),
            pltpu.VMEM((2, head_count, 2, rows + 2) + cell, bf),
            pltpu.VMEM((2, tall_count, 2, columns) + cell, bf),
            pltpu.VMEM((tall_count, columns) + cell, bf),
            pltpu.VMEM((tall_count, columns) + cell, bf),
            pltpu.VMEM((feature // unit, queries, unit), bf),
            pltpu.VMEM((ha_count, queries, inputs.shape[3]), bf),
            pltpu.VMEM((ha_count, slice_columns // unit, queries, unit), bf),
            pltpu.VMEM((chips, 2) + part, bf),
            pltpu.VMEM((chips,) + part, bf),
            pltpu.VMEM((chips,) + part, bf),
            pltpu.VMEM((halves,) + part, bf),
            pltpu.VMEM((halves,) + part, bf),
            pltpu.VMEM((halves,) + part, bf),
            dma((1,)),
            dma((2, 2, 2, tall_runs)),
            dma((2, 2, 2, tall_runs)),
            dma((2, tall_runs)),
            dma((2, tall_runs)),
            dma((2, runs)),
            dma((2, runs)),
            dma((2, tall_runs)),
            dma((2, tall_runs)),
            dma((2, runs)),
            dma((2, runs)),
            dma((ha_count, CHUNKS)),
            dma((ha_count, CHUNKS)),
            dma((ha_count // 2, CHUNKS)),
            dma((ha_count,)),
            dma((ha_count,)),
            dma((chips,)),
            dma((chips,)),
            dma((halves,)),
            dma((halves,)),
            dma((halves,)),
            dma((halves,)),
        ],
        compiler_params=pltpu.CompilerParams(
            collective_id=which, has_side_effects=True, vmem_limit_bytes=56 * 1024 * 1024
        ),
    )(
        window.T,
        tokens(query_vectors),
        tokens(output_cotangent),
        cells(key_vectors),
        cells(value_vectors),
        tokens(inputs),
    )

    def to_grid(x):
        return x.transpose(2, 0, 1, 3)

    return (att.reshape(query_vectors.shape), to_grid(dk), to_grid(dv), weight_gradient)


def by_reach(*args):
    reaching = jnp.sum(args[5][:, 2])
    which = sum((reaching > most).astype(jnp.int32) for most in TALLS[:-1])
    branches = [functools.partial(on_device, at) for at in range(len(TALLS))]
    return lax.switch(which, branches, *args)


def solution(mesh):
    cells = P(None, "ha", "wa", None)
    return jax.shard_map(
        by_reach,
        mesh=mesh,
        in_specs=(cells, cells, cells, cells, cells, P()),
        out_specs=(cells, cells, cells, P("wa", "ha")),
        check_vma=False,
    )
```

```python
import functools
import math

import jax
import jax.numpy as jnp
from jax import lax
from jax.experimental import pallas as pl
from jax.experimental.pallas import tpu as pltpu
from jax.sharding import PartitionSpec as P

MESH = pl.DeviceIdType.MESH
TALLS = (6, 8, 12)
BATCH = 3
CHUNKS = 4
HIDDEN = -1e30
FRAME_KINDS = ((1, 0), (1, 1), (1, 2), (2, 0), (2, 1))


def split(low, high):
    count = high - low
    runs = -(-count // BATCH)
    out = []
    for at in range(runs):
        size = count // runs + (1 if at < count % runs else 0)
        out.append((low, size))
        low += size
    return out


def attention_kernel(
    tall_count,
    window_ref,
    q_ref,
    do_ref,
    k_ref,
    v_ref,
    x_ref,
    att_ref,
    dk_ref,
    dv_ref,
    weight_ref,
    order_ref,
    pos_ref,
    kind_ref,
    code_ref,
    heads_kv,
    heads_q,
    heads_do,
    padded,
    terms,
    att_slots,
    dq_slots,
    from_side,
    from_row,
    relay_rows,
    relay_terms,
    slopes_own,
    x_all,
    slopes_all,
    product,
    from_partner,
    pair_sums,
    from_pair,
    chip_sums,
    from_chips,
    own_x_sem,
    row_send,
    row_recv,
    relay_send,
    relay_recv,
    col_send,
    col_recv,
    corner_send,
    corner_recv,
    side_send,
    side_recv,
    x_send,
    x_recv,
    forward_send,
    slope_send,
    slope_recv,
    core_send,
    core_recv,
    pair_send,
    pair_recv,
    chip_send,
    chip_recv,
):
    rows, columns, frames, _ = k_ref.shape
    head_count = padded.shape[0]
    head_size = padded.shape[-1]
    queries = q_ref.shape[0]
    bf = jnp.bfloat16
    scale = 1.0 / math.sqrt(head_size)
    ha_count, wa_count = lax.axis_size("ha"), lax.axis_size("wa")
    ha, wa = lax.axis_index("ha"), lax.axis_index("wa")
    flat_count = head_count - tall_count
    flat_runs = split(0, flat_count)
    tall_runs = split(flat_count, head_count)
    runs = flat_runs + tall_runs
    place = {"ha": ha, "wa": wa}
    exists = {
        ("ha", -1): ha > 0,
        ("ha", 1): ha < ha_count - 1,
        ("wa", -1): wa > 0,
        ("wa", 1): wa < wa_count - 1,
    }
    above, below = rows, rows + 1
    left, right = columns, columns + 1
    low, high = ha % 2, ha // 2
    partner = 2 * high + 1 - low
    pairs = ha_count // 2
    relayed = pairs == 2

    tall_slots = pl.ds(flat_count, tall_count)
    for at, side, line in ((0, 0, above), (ha_count - 1, 1, below)):

        @pl.when(ha == at)
        def _(side=side, line=line):
            hidden = padded.at[tall_slots, :, line]
            hidden[...] = jnp.zeros(hidden.shape, bf)
            from_row[side] = jnp.zeros(from_row.shape[1:], bf)

    for at, side, line in ((0, 0, left), (wa_count - 1, 1, right)):

        @pl.when(wa == at)
        def _(side=side, line=line):
            for count, first, lines in (
                (flat_count, 0, rows),
                (tall_count, flat_count, rows + 2),
            ):
                if count:
                    hidden = padded.at[pl.ds(first, count), :, pl.ds(0, lines), line]
                    hidden[...] = jnp.zeros(hidden.shape, bf)
                    fold = from_side.at[side, pl.ds(first, count), :, pl.ds(0, lines)]
                    fold[...] = jnp.zeros(fold.shape, bf)

    barrier = pltpu.get_barrier_semaphore()
    for axis, count in (("ha", ha_count), ("wa", wa_count)):
        for step in range(1, count):
            pl.semaphore_signal(
                barrier,
                inc=1,
                device_id={axis: (place[axis] + step) % count},
                device_id_type=MESH,
            )
    own_x = pltpu.make_async_copy(x_ref, x_all.at[ha], own_x_sem.at[0])
    own_x.start()

    reach = [window_ref[2, head] for head in range(head_count)]
    next_tall = head_count - sum(reach)
    next_flat = 0
    spots = []
    for head in range(head_count):
        spot = jnp.where(reach[head] > 0, next_tall, next_flat)
        next_tall = next_tall + reach[head]
        next_flat = next_flat + 1 - reach[head]
        pos_ref[head] = spot
        spots.append(spot)
    kinds = []
    for head in range(head_count):
        tile = jnp.where(window_ref[0, head] == 2, 3, 0) + window_ref[1, head]
        kinds.append(4 * tile + 2 * reach[head] + window_ref[3, head])
    for slot in range(head_count):
        here = [spots[head] == slot for head in range(head_count)]
        order_ref[slot] = sum(jnp.where(here[head], head, 0) for head in range(head_count))
        kind_ref[slot] = sum(jnp.where(here[head], kinds[head], 0) for head in range(head_count))

    for head in range(head_count):
        lanes = slice(head * head_size, (head + 1) * head_size)
        heads_kv[head, 0] = k_ref[:, :, :, lanes]
        heads_kv[head, 1] = v_ref[:, :, :, lanes]
    for slot in range(head_count):
        padded[slot, :, :rows, :columns] = heads_kv[order_ref[slot]]

    pl.semaphore_wait(barrier, ha_count + wa_count - 2)

    def remote(source, target, send, recv, axis, device):
        return pltpu.make_async_remote_copy(
            src_ref=source,
            dst_ref=target,
            send_sem=send,
            recv_sem=recv,
            device_id={axis: device},
            device_id_type=MESH,
        )

    def landed(buffer, sem):
        pltpu.make_async_copy(buffer, buffer, sem).wait()

    def detour(by):
        if not relayed:
            return None
        return ha == (1 if by > 0 else pairs)

    def row_source(kind, by, part, run):
        first, size = tall_runs[run]
        if kind == 0:
            return padded.at[
                pl.ds(first, size), part, 0 if by < 0 else rows - 1, pl.ds(0, columns)
            ]
        return terms.at[
            pl.ds(first, size), part, above if by < 0 else below, pl.ds(0, columns)
        ]

    def row_target(kind, by, part, run):
        first, size = tall_runs[run]
        if kind == 0:
            return padded.at[
                pl.ds(first, size), part, below if by < 0 else above, pl.ds(0, columns)
            ]
        return from_row.at[1 if by < 0 else 0, pl.ds(first - flat_count, size), part]

    def relay_buffer(kind, run):
        first, size = tall_runs[run]
        return (relay_rows, relay_terms)[kind].at[pl.ds(first - flat_count, size)]

    def row_copy(kind, by, part, run):
        side = 0 if by < 0 else 1
        return remote(
            row_source(kind, by, part, run),
            row_target(kind, by, part, run),
            row_send.at[kind, side, part, run],
            row_recv.at[kind, side, part, run],
            "ha",
            ha + by,
        )

    def detour_copy(kind, by, run):
        side = 0 if by < 0 else 1
        return remote(
            row_source(kind, by, 1, run),
            relay_buffer(kind, run),
            row_send.at[kind, side, 1, run],
            relay_recv.at[kind, run],
            "ha",
            (ha + 2) % ha_count,
        )

    def relay_copy(kind, by, run):
        side = 0 if by < 0 else 1
        return remote(
            relay_buffer(kind, run),
            row_target(kind, by, 1, run),
            relay_send.at[kind, run],
            row_recv.at[kind, side, 1, run],
            "ha",
            partner,
        )

    def each_row_copy(kind, run, act):
        for by in (-1, 1):
            turn = detour(by)
            for part in range(2):
                direct = exists["ha", by]
                if part == 1 and turn is not None:
                    direct = direct & jnp.logical_not(turn)

                    @pl.when(turn)
                    def _(by=by):
                        act(detour_copy(kind, by, run))

                @pl.when(direct)
                def _(by=by, part=part):
                    act(row_copy(kind, by, part, run))

    def start_rows(kind, run):
        each_row_copy(kind, run, lambda copy: copy.start())

    def relay(kind, run):
        if relayed:
            for at, by in ((0, -1), (ha_count - 1, 1)):

                @pl.when(ha == at)
                def _(by=by):
                    landed(relay_buffer(kind, run), relay_recv.at[kind, run])
                    relay_copy(kind, by, run).start()

    def rows_arrived(kind, run):
        for by in (-1, 1):

            @pl.when(exists["ha", -by])
            def _(by=by):
                for part in range(2):
                    row_copy(kind, by, part, run).wait_recv()

    def column_copy(kind, by, run):
        first, size = (tall_runs if kind == 1 else runs)[run]
        slots = pl.ds(first, size)
        side = 0 if by < 0 else 1
        if kind == 2:
            lines = pl.ds(0, rows if first < flat_count else rows + 2)
            source = terms.at[slots, :, lines, left if by < 0 else right]
            target = from_side.at[1 if by < 0 else 0, slots, :, lines]
        else:
            lines = pl.ds(0, rows) if kind == 0 else pl.ds(rows, 2)
            source = padded.at[slots, :, lines, 0 if by < 0 else columns - 1]
            target = padded.at[slots, :, lines, right if by < 0 else left]
        send = (col_send, corner_send, side_send)[kind]
        recv = (col_recv, corner_recv, side_recv)[kind]
        return remote(source, target, send.at[side, run], recv.at[side, run], "wa", wa + by)

    def start_columns(kind, run):
        for by in (-1, 1):

            @pl.when(exists["wa", by])
            def _(by=by):
                column_copy(kind, by, run).start()

    def columns_arrived(kind, run):
        for by in (-1, 1):

            @pl.when(exists["wa", -by])
            def _(by=by):
                column_copy(kind, by, run).wait_recv()

    chunk = queries // CHUNKS

    def x_copy(peer, part):
        tokens = pl.ds(part * chunk, chunk)
        return remote(
            x_ref.at[tokens],
            x_all.at[ha, tokens],
            x_send.at[peer, part],
            x_recv.at[ha, part],
            "ha",
            peer,
        )

    last = CHUNKS - 1

    def back_copy(pair):
        tokens = pl.ds(last * chunk, chunk)
        return remote(
            x_all.at[2 * pair + low, tokens],
            x_all.at[2 * pair + low, tokens],
            forward_send.at[pair, last],
            x_recv.at[2 * pair + low, last],
            "ha",
            partner,
        )

    def forward_copy(pair, part):
        tokens = pl.ds(part * chunk, chunk)
        return remote(
            x_all.at[partner, tokens],
            x_all.at[partner, tokens],
            forward_send.at[pair, part],
            x_recv.at[partner, part],
            "ha",
            2 * pair + low,
        )

    def x_landed(peer, part):
        tokens = pl.ds(part * chunk, chunk)
        landed(x_all.at[peer, tokens], x_recv.at[peer, part])

    def other_pairs(act):
        for pair in range(pairs):

            @pl.when(pair != high)
            def _(pair=pair):
                act(pair)

    for run in range(len(tall_runs)):
        start_rows(0, run)
    start_columns(0, 0)
    for part in range(CHUNKS):
        other_pairs(lambda pair: x_copy(2 * pair + low, part).start())

    query_id = lax.broadcasted_iota(jnp.int32, (1, queries), 1)
    key_id = lax.broadcasted_iota(jnp.int32, (code_ref.shape[0], 1), 0)
    query_frame = query_id // (rows * columns)
    query_row = (query_id // columns) % rows
    query_column = query_id % columns
    key_frame = key_id % frames
    key_row = key_id // (frames * (columns + 2))
    key_column = (key_id // frames) % (columns + 2)
    key_row = jnp.where(key_row == above, -1, jnp.where(key_row == below, rows, key_row))
    key_column = jnp.where(
        key_column == left, -1, jnp.where(key_column == right, columns, key_column)
    )
    outside = (
        (key_row + ha * rows < 0)
        | (key_row + ha * rows >= ha_count * rows)
        | (key_column + wa * columns < 0)
        | (key_column + wa * columns >= wa_count * columns)
    )
    key_row = jnp.where(outside, 1000, key_row)
    row_gap = jnp.abs(query_row - key_row)
    column_gap = jnp.abs(query_column - key_column)
    cells = jnp.zeros(code_ref.shape, jnp.int32)
    for row_reach in range(2):
        for column_reach in range(2):
            near = (row_gap <= row_reach) & (column_gap <= column_reach)
            cells = cells | jnp.where(near, 1 << (2 * row_reach + column_reach), 0)
    code = jnp.zeros(code_ref.shape, jnp.int32)
    for kind, (tile, frame_reach) in enumerate(FRAME_KINDS):
        gap = jnp.abs(query_frame // tile - key_frame // tile)
        code = code | jnp.where(gap <= frame_reach, cells << (4 * kind), 0)
    code_ref[...] = code
    for head in range(head_count):
        lanes = slice(head * head_size, (head + 1) * head_size)
        heads_q[head] = q_ref[:, lanes]
        heads_do[head] = do_ref[:, lanes]
    for run in range(1, len(runs)):
        start_columns(0, run)

    across = (((1,), (1,)), ((), ()))
    down = (((0,), (0,)), ((), ()))
    dot = functools.partial(lax.dot_general, preferred_element_type=jnp.float32)
    lift = scale * math.log2(math.e)

    def attend(run):
        first, size = runs[run]
        lines = rows if first < flat_count else rows + 2
        keys = lines * (columns + 2) * frames
        slots = range(first, first + size)
        q = [heads_q[order_ref[slot]] for slot in slots]
        do = [heads_do[order_ref[slot]] for slot in slots]
        k = [padded[slot, 0, :lines].reshape(keys, head_size) for slot in slots]
        v = [padded[slot, 1, :lines].reshape(keys, head_size) for slot in slots]
        bits = [jnp.left_shift(1, kind_ref[slot]) for slot in slots]
        each = range(size)
        scores = [dot(k[i], q[i], across) for i in each]
        upstream = [dot(v[i], do[i], across) for i in each]
        scores = [
            jnp.where((code_ref[:keys] & bits[i]) != 0, scores[i], HIDDEN) for i in each
        ]
        top = [jnp.max(scores[i], axis=0, keepdims=True) for i in each]
        lifted = [jnp.exp2((scores[i] - top[i]) * lift) for i in each]
        total = [jnp.sum(lifted[i], axis=0, keepdims=True) for i in each]
        weight = [(lifted[i] * (1.0 / total[i])).astype(bf) for i in each]
        wide = [weight[i].astype(jnp.float32) for i in each]
        delta = [jnp.sum(wide[i] * upstream[i], axis=0, keepdims=True) for i in each]
        slopes = [(wide[i] * (upstream[i] - delta[i])).astype(bf) for i in each]
        shape = (lines,) + terms.shape[3:]
        for i, slot in enumerate(slots):
            dv = jnp.dot(weight[i], do[i], preferred_element_type=jnp.float32)
            terms[slot, 1, :lines] = dv.astype(bf).reshape(shape)
            dk = jnp.dot(slopes[i], q[i], preferred_element_type=jnp.float32) * scale
            terms[slot, 0, :lines] = dk.astype(bf).reshape(shape)
            att_slots[slot] = dot(weight[i], v[i], down).astype(bf)
            dq_slots[slot] = (dot(slopes[i], k[i], down) * scale).astype(bf)

    tall_base = len(flat_runs)
    opened = 0

    def open_tall(run):
        relay(0, run)
        rows_arrived(0, run)
        start_columns(1, run)

    def pass_on(part):
        x_landed(partner, part)
        other_pairs(lambda pair: forward_copy(pair, part).start())

    passed = 0
    for run in range(len(runs)):
        columns_arrived(0, run)
        if run >= tall_base:
            while opened < min(run - tall_base + 2, len(tall_runs)):
                open_tall(opened)
                opened += 1
            columns_arrived(1, run - tall_base)
        attend(run)
        start_columns(2, run)
        if run < CHUNKS:
            x_copy(partner, run).start()
        if run < tall_base and opened < len(tall_runs):
            open_tall(opened)
            opened += 1
        if run >= 2 and passed < last:
            pass_on(passed)
            passed += 1
    for part in range(len(runs), CHUNKS):
        x_copy(partner, part).start()

    unit = slopes_own.shape[2]
    share = slopes_all.shape[1]
    pieces = head_size // unit
    for head in range(head_count):
        value = dq_slots[pos_ref[head]]
        for piece in range(pieces):
            slopes_own[head * pieces + piece] = value[:, piece * unit : (piece + 1) * unit]

    def slope_copy(peer):
        return remote(
            slopes_own.at[pl.ds(peer * share, share)],
            slopes_all.at[ha],
            slope_send.at[peer],
            slope_recv.at[ha],
            "ha",
            peer,
        )

    for peer in range(ha_count):

        @pl.when(peer != ha)
        def _(peer=peer):
            slope_copy(peer).start()

        @pl.when(peer == ha)
        def _(peer=peer):
            slopes_all[peer] = slopes_own[pl.ds(peer * share, share)]

    for part in range(passed, last):
        pass_on(part)

    def back(pair):
        x_landed(2 * pair + low, last)
        back_copy(pair).start()

    other_pairs(back)
    x_landed(partner, last)

    for head in range(head_count):
        att_ref[:, head * head_size : (head + 1) * head_size] = att_slots[pos_ref[head]]

    def fold_sides(run):
        first, size = runs[run]
        slots = pl.ds(first, size)
        lines = rows if first < flat_count else rows + 2
        columns_arrived(2, run)
        for side, line in ((0, 0), (1, columns - 1)):
            terms[slots, :, :lines, line] = (
                terms[slots, :, :lines, line] + from_side[side, slots, :, :lines]
            )

    for run in range(len(flat_runs)):
        fold_sides(run)

    own_x.wait()
    for peer in range(ha_count):

        @pl.when(peer != ha)
        def _(peer=peer):
            landed(slopes_all.at[peer], slope_recv.at[peer])

    def wait_others(pair):
        for part in range(CHUNKS):
            if part < last:
                x_landed(2 * pair + low, part)
            x_landed(2 * pair + 1 - low, part)

    other_pairs(wait_others)

    core, chip = wa % 2, wa // 2
    chips = wa_count // 2
    halves = chips // 2
    parity, own_half = chip % 2, chip // 2
    block = x_all.shape[2] // chips
    tokens = ha_count * queries
    aligned = block % 128 == 0

    def core_copy(dest):
        return remote(
            product.at[dest, 1 - core],
            from_partner.at[dest],
            core_send.at[dest],
            core_recv.at[dest],
            "wa",
            wa + 1 - 2 * core,
        )

    def pair_copy(half):
        return remote(
            pair_sums.at[2 * half + 1 - parity],
            from_pair.at[half],
            pair_send.at[half],
            pair_recv.at[half],
            "wa",
            2 * (chip + 1 - 2 * parity) + core,
        )

    def chip_copy(half):
        return remote(
            chip_sums.at[half],
            from_chips.at[own_half],
            chip_send.at[half],
            chip_recv.at[own_half],
            "wa",
            2 * (2 * half + parity) + core,
        )

    stations = []
    for step in range(halves):
        half = lax.rem(own_half + 1 + step, halves)
        stations += [2 * half + 1 - parity, 2 * half + parity]
    columns_of = [slopes_all[:, at].reshape(tokens, unit) for at in range(share)]
    slope_block = columns_of[0] if share == 1 else jnp.concatenate(columns_of, axis=1)
    for step in range(chips):
        if aligned:
            dest = stations[step]
            token_block = x_all[:, :, pl.ds(pl.multiple_of(dest * block, block), block)]
        else:
            dest = step
            token_block = x_all[:, :, step * block : (step + 1) * block]
        value = dot(token_block.reshape(tokens, block), slope_block, down)
        product[dest] = value.astype(bf).reshape(product.shape[1:])
        core_copy(dest).start()

    for run in range(len(tall_runs)):
        fold_sides(tall_base + run)
        start_rows(1, run)

    for step in range(halves):
        half = lax.rem(own_half + 1 + step, halves)
        for dest in (2 * half + 1 - parity, 2 * half + parity):
            core_copy(dest).wait_recv()
            both = product[dest, core].astype(jnp.float32) + from_partner[dest].astype(
                jnp.float32
            )
            pair_sums[dest] = both.astype(bf)
        pair_copy(half).start()

    for run in range(len(tall_runs)):
        relay(1, run)

    for step in range(halves):
        half = lax.rem(own_half + 1 + step, halves)
        pair_copy(half).wait_recv()
        both = pair_sums[2 * half + parity].astype(jnp.float32) + from_pair[half].astype(
            jnp.float32
        )
        chip_sums[half] = both.astype(bf)
        if step < halves - 1:
            chip_copy(half).start()
        else:
            from_chips[half] = chip_sums[half]

    for run in range(len(tall_runs)):
        rows_arrived(1, run)
        first, size = tall_runs[run]
        slots = pl.ds(first, size)
        near = pl.ds(first - flat_count, size)
        for side, line in ((0, 0), (1, rows - 1)):
            terms[slots, :, line, :columns] = (
                terms[slots, :, line, :columns] + from_row[side, near]
            )

    for head in range(head_count):
        here = slice(head * head_size, (head + 1) * head_size)
        dk_ref[:, :, :, here] = terms[pos_ref[head], 0, :rows, :columns]
        dv_ref[:, :, :, here] = terms[pos_ref[head], 1, :rows, :columns]

    for step in range(halves - 1):
        half = lax.rem(own_half + 1 + step, halves)
        landed(from_chips.at[half], chip_recv.at[half])
    gathered = from_chips[0].astype(jnp.float32)
    for half in range(1, halves):
        gathered = gathered + from_chips[half].astype(jnp.float32)
    tokens_all = queries * ha_count * wa_count
    weight_ref[...] = (gathered * (1.0 / math.sqrt(tokens_all))).astype(weight_ref.dtype)

    for kind in range(2):
        for run in range(len(tall_runs)):
            each_row_copy(kind, run, lambda copy: copy.wait_send())
            if relayed:
                for at, by in ((0, -1), (ha_count - 1, 1)):

                    @pl.when(ha == at)
                    def _(by=by, kind=kind, run=run):
                        relay_copy(kind, by, run).wait_send()

    for kind, count in ((0, len(runs)), (1, len(tall_runs)), (2, len(runs))):
        for run in range(count):
            for by in (-1, 1):

                @pl.when(exists["wa", by])
                def _(by=by, kind=kind, run=run):
                    column_copy(kind, by, run).wait_send()

    def x_sent(pair):
        for part in range(CHUNKS):
            x_copy(2 * pair + low, part).wait_send()
            (forward_copy(pair, part) if part < last else back_copy(pair)).wait_send()

    for part in range(CHUNKS):
        x_copy(partner, part).wait_send()
    other_pairs(x_sent)
    for peer in range(ha_count):

        @pl.when(peer != ha)
        def _(peer=peer):
            slope_copy(peer).wait_send()

    for dest in range(chips):
        core_copy(dest).wait_send()
    for half in range(halves):
        pair_copy(half).wait_send()
    for step in range(halves - 1):
        chip_copy(lax.rem(own_half + 1 + step, halves)).wait_send()


def on_device(
    which, inputs, query_vectors, key_vectors, value_vectors, output_cotangent, window
):
    tall_count = TALLS[which]
    frames, rows, columns, feature = query_vectors.shape
    head_count = window.shape[0]
    head_size = feature // head_count
    queries = frames * rows * columns
    bf = jnp.bfloat16

    def tokens(x):
        return x.reshape(queries, x.shape[3])

    def cells(x):
        return x.transpose(1, 2, 0, 3)

    ha_count, wa_count = lax.axis_size("ha"), lax.axis_size("wa")
    chips = wa_count // 2
    halves = chips // 2
    slice_rows = inputs.shape[3] // wa_count
    slice_columns = feature // ha_count
    unit = math.gcd(head_size, slice_columns)
    cell = (frames, head_size)
    tall = (head_count, 2, rows + 2, columns + 2) + cell
    keys = (rows + 2) * (columns + 2) * frames
    part = (slice_rows, slice_columns)
    tall_runs = len(split(head_count - tall_count, head_count))
    runs = len(split(0, head_count - tall_count)) + tall_runs
    vmem = pl.BlockSpec(memory_space=pltpu.VMEM)
    dma = pltpu.SemaphoreType.DMA
    buffers = [
        pltpu.VMEM((keys, queries), jnp.int32),
        pltpu.VMEM((head_count, 2, rows, columns) + cell, bf),
        pltpu.VMEM((head_count, queries, head_size), bf),
        pltpu.VMEM((head_count, queries, head_size), bf),
        pltpu.VMEM(tall, bf),
        pltpu.VMEM(tall, bf),
        pltpu.VMEM((head_count, queries, head_size), bf),
        pltpu.VMEM((head_count, queries, head_size), bf),
        pltpu.VMEM((2, head_count, 2, rows + 2) + cell, bf),
        pltpu.VMEM((2, tall_count, 2, columns) + cell, bf),
        pltpu.VMEM((tall_count, columns) + cell, bf),
        pltpu.VMEM((tall_count, columns) + cell, bf),
        pltpu.VMEM((feature // unit, queries, unit), bf),
        pltpu.VMEM((ha_count, queries, inputs.shape[3]), bf),
        pltpu.VMEM((ha_count, slice_columns // unit, queries, unit), bf),
        pltpu.VMEM((chips, 2) + part, bf),
        pltpu.VMEM((chips,) + part, bf),
        pltpu.VMEM((chips,) + part, bf),
        pltpu.VMEM((halves,) + part, bf),
        pltpu.VMEM((halves,) + part, bf),
        pltpu.VMEM((halves,) + part, bf),
    ]
    held = sum(
        math.prod(buffer.shape) * jnp.dtype(buffer.dtype).itemsize for buffer in buffers
    )
    held += 10 * queries * feature * 2
    att, dk, dv, weight_gradient = pl.pallas_call(
        functools.partial(attention_kernel, tall_count),
        out_shape=(
            jax.ShapeDtypeStruct((queries, feature), bf),
            jax.ShapeDtypeStruct((rows, columns, frames, feature), bf),
            jax.ShapeDtypeStruct((rows, columns, frames, feature), bf),
            jax.ShapeDtypeStruct(part, bf),
        ),
        in_specs=[pl.BlockSpec(memory_space=pltpu.SMEM), vmem, vmem, vmem, vmem, vmem],
        out_specs=(vmem, vmem, vmem, vmem),
        scratch_shapes=[
            pltpu.SMEM((head_count,), jnp.int32),
            pltpu.SMEM((head_count,), jnp.int32),
            pltpu.SMEM((head_count,), jnp.int32),
            *buffers,
            dma((1,)),
            dma((2, 2, 2, tall_runs)),
            dma((2, 2, 2, tall_runs)),
            dma((2, tall_runs)),
            dma((2, tall_runs)),
            dma((2, runs)),
            dma((2, runs)),
            dma((2, tall_runs)),
            dma((2, tall_runs)),
            dma((2, runs)),
            dma((2, runs)),
            dma((ha_count, CHUNKS)),
            dma((ha_count, CHUNKS)),
            dma((ha_count // 2, CHUNKS)),
            dma((ha_count,)),
            dma((ha_count,)),
            dma((chips,)),
            dma((chips,)),
            dma((halves,)),
            dma((halves,)),
            dma((halves,)),
            dma((halves,)),
        ],
        compiler_params=pltpu.CompilerParams(
            collective_id=which, has_side_effects=True, vmem_limit_bytes=held + 4 * 1024 * 1024
        ),
    )(
        window.T,
        tokens(query_vectors),
        tokens(output_cotangent),
        cells(key_vectors),
        cells(value_vectors),
        tokens(inputs),
    )

    def to_grid(x):
        return x.transpose(2, 0, 1, 3)

    return (att.reshape(query_vectors.shape), to_grid(dk), to_grid(dv), weight_gradient)


def by_reach(*args):
    reaching = jnp.sum(args[5][:, 2])
    which = sum((reaching > most).astype(jnp.int32) for most in TALLS[:-1])
    branches = [functools.partial(on_device, at) for at in range(len(TALLS))]
    return lax.switch(which, branches, *args)


def solution(mesh):
    cells = P(None, "ha", "wa", None)
    return jax.shard_map(
        by_reach,
        mesh=mesh,
        in_specs=(cells, cells, cells, cells, cells, P()),
        out_specs=(cells, cells, cells, P("wa", "ha")),
        check_vma=False,
    )
```

```python
import functools
import math

import jax
import jax.numpy as jnp
from jax import lax
from jax.experimental import pallas as pl
from jax.experimental.pallas import tpu as pltpu
from jax.sharding import PartitionSpec as P

MESH = pl.DeviceIdType.MESH
TALLS = (6, 8, 12)
BATCH = 3
CHUNKS = 4
HIDDEN = -1e30
FRAME_KINDS = ((1, 0), (1, 1), (1, 2), (2, 0), (2, 1))


def split(low, high):
    count = high - low
    runs = -(-count // BATCH)
    out = []
    for at in range(runs):
        size = count // runs + (1 if at < count % runs else 0)
        out.append((low, size))
        low += size
    return out


def attention_kernel(
    tall_count,
    window_ref,
    q_ref,
    do_ref,
    k_ref,
    v_ref,
    x_ref,
    att_ref,
    dk_ref,
    dv_ref,
    weight_ref,
    order_ref,
    pos_ref,
    kind_ref,
    code_ref,
    heads_kv,
    heads_q,
    heads_do,
    padded,
    terms,
    att_slots,
    dq_slots,
    from_side,
    from_row,
    relay_rows,
    relay_terms,
    slopes_own,
    x_all,
    slopes_all,
    product,
    from_partner,
    pair_sums,
    from_pair,
    chip_sums,
    from_chips,
    own_x_sem,
    row_send,
    row_recv,
    relay_send,
    relay_recv,
    col_send,
    col_recv,
    corner_send,
    corner_recv,
    side_send,
    side_recv,
    x_send,
    x_recv,
    forward_send,
    slope_send,
    slope_recv,
    core_send,
    core_recv,
    pair_send,
    pair_recv,
    chip_send,
    chip_recv,
):
    rows, columns, frames, _ = k_ref.shape
    head_count = padded.shape[0]
    head_size = padded.shape[-1]
    queries = q_ref.shape[0]
    bf = jnp.bfloat16
    scale = 1.0 / math.sqrt(head_size)
    ha_count, wa_count = lax.axis_size("ha"), lax.axis_size("wa")
    ha, wa = lax.axis_index("ha"), lax.axis_index("wa")
    flat_count = head_count - tall_count
    flat_runs = split(0, flat_count)
    tall_runs = split(flat_count, head_count)
    runs = flat_runs + tall_runs
    place = {"ha": ha, "wa": wa}
    exists = {
        ("ha", -1): ha > 0,
        ("ha", 1): ha < ha_count - 1,
        ("wa", -1): wa > 0,
        ("wa", 1): wa < wa_count - 1,
    }
    above, below = rows, rows + 1
    left, right = columns, columns + 1
    low, high = ha % 2, ha // 2
    partner = 2 * high + 1 - low
    pairs = ha_count // 2
    relayed = pairs == 2

    tall_slots = pl.ds(flat_count, tall_count)
    for at, side, line in ((0, 0, above), (ha_count - 1, 1, below)):

        @pl.when(ha == at)
        def _(side=side, line=line):
            hidden = padded.at[tall_slots, :, line]
            hidden[...] = jnp.zeros(hidden.shape, bf)
            from_row[side] = jnp.zeros(from_row.shape[1:], bf)

    for at, side, line in ((0, 0, left), (wa_count - 1, 1, right)):

        @pl.when(wa == at)
        def _(side=side, line=line):
            for count, first, lines in (
                (flat_count, 0, rows),
                (tall_count, flat_count, rows + 2),
            ):
                if count:
                    hidden = padded.at[pl.ds(first, count), :, pl.ds(0, lines), line]
                    hidden[...] = jnp.zeros(hidden.shape, bf)
                    fold = from_side.at[side, pl.ds(first, count), :, pl.ds(0, lines)]
                    fold[...] = jnp.zeros(fold.shape, bf)

    barrier = pltpu.get_barrier_semaphore()
    for axis, count in (("ha", ha_count), ("wa", wa_count)):
        for step in range(1, count):
            pl.semaphore_signal(
                barrier,
                inc=1,
                device_id={axis: (place[axis] + step) % count},
                device_id_type=MESH,
            )
    own_x = pltpu.make_async_copy(x_ref, x_all.at[ha], own_x_sem.at[0])
    own_x.start()

    reach = [window_ref[2, head] for head in range(head_count)]
    next_tall = head_count - sum(reach)
    next_flat = 0
    spots = []
    for head in range(head_count):
        spot = jnp.where(reach[head] > 0, next_tall, next_flat)
        next_tall = next_tall + reach[head]
        next_flat = next_flat + 1 - reach[head]
        pos_ref[head] = spot
        spots.append(spot)
    kinds = []
    for head in range(head_count):
        tile = jnp.where(window_ref[0, head] == 2, 3, 0) + window_ref[1, head]
        kinds.append(4 * tile + 2 * reach[head] + window_ref[3, head])
    for slot in range(head_count):
        here = [spots[head] == slot for head in range(head_count)]
        order_ref[slot] = sum(jnp.where(here[head], head, 0) for head in range(head_count))
        kind_ref[slot] = sum(jnp.where(here[head], kinds[head], 0) for head in range(head_count))

    for head in range(head_count):
        lanes = slice(head * head_size, (head + 1) * head_size)
        heads_kv[head, 0] = k_ref[:, :, :, lanes]
        heads_kv[head, 1] = v_ref[:, :, :, lanes]
    for slot in range(head_count):
        padded[slot, :, :rows, :columns] = heads_kv[order_ref[slot]]

    pl.semaphore_wait(barrier, ha_count + wa_count - 2)

    def remote(source, target, send, recv, axis, device):
        return pltpu.make_async_remote_copy(
            src_ref=source,
            dst_ref=target,
            send_sem=send,
            recv_sem=recv,
            device_id={axis: device},
            device_id_type=MESH,
        )

    def landed(buffer, sem):
        pltpu.make_async_copy(buffer, buffer, sem).wait()

    def detour(by):
        if not relayed:
            return None
        return ha == (1 if by > 0 else pairs)

    def row_source(kind, by, part, run):
        first, size = tall_runs[run]
        if kind == 0:
            return padded.at[
                pl.ds(first, size), part, 0 if by < 0 else rows - 1, pl.ds(0, columns)
            ]
        return terms.at[
            pl.ds(first, size), part, above if by < 0 else below, pl.ds(0, columns)
        ]

    def row_target(kind, by, part, run):
        first, size = tall_runs[run]
        if kind == 0:
            return padded.at[
                pl.ds(first, size), part, below if by < 0 else above, pl.ds(0, columns)
            ]
        return from_row.at[1 if by < 0 else 0, pl.ds(first - flat_count, size), part]

    def relay_buffer(kind, run):
        first, size = tall_runs[run]
        return (relay_rows, relay_terms)[kind].at[pl.ds(first - flat_count, size)]

    def row_copy(kind, by, part, run):
        side = 0 if by < 0 else 1
        return remote(
            row_source(kind, by, part, run),
            row_target(kind, by, part, run),
            row_send.at[kind, side, part, run],
            row_recv.at[kind, side, part, run],
            "ha",
            ha + by,
        )

    def detour_copy(kind, by, run):
        side = 0 if by < 0 else 1
        return remote(
            row_source(kind, by, 1, run),
            relay_buffer(kind, run),
            row_send.at[kind, side, 1, run],
            relay_recv.at[kind, run],
            "ha",
            (ha + 2) % ha_count,
        )

    def relay_copy(kind, by, run):
        side = 0 if by < 0 else 1
        return remote(
            relay_buffer(kind, run),
            row_target(kind, by, 1, run),
            relay_send.at[kind, run],
            row_recv.at[kind, side, 1, run],
            "ha",
            partner,
        )

    def each_row_copy(kind, run, act):
        for by in (-1, 1):
            turn = detour(by)
            for part in range(2):
                direct = exists["ha", by]
                if part == 1 and turn is not None:
                    direct = direct & jnp.logical_not(turn)

                    @pl.when(turn)
                    def _(by=by):
                        act(detour_copy(kind, by, run))

                @pl.when(direct)
                def _(by=by, part=part):
                    act(row_copy(kind, by, part, run))

    def start_rows(kind, run):
        each_row_copy(kind, run, lambda copy: copy.start())

    def relay(kind, run):
        if relayed:
            for at, by in ((0, -1), (ha_count - 1, 1)):

                @pl.when(ha == at)
                def _(by=by):
                    landed(relay_buffer(kind, run), relay_recv.at[kind, run])
                    relay_copy(kind, by, run).start()

    def rows_arrived(kind, run):
        for by in (-1, 1):

            @pl.when(exists["ha", -by])
            def _(by=by):
                for part in range(2):
                    row_copy(kind, by, part, run).wait_recv()

    def column_copy(kind, by, run):
        first, size = (tall_runs if kind == 1 else runs)[run]
        slots = pl.ds(first, size)
        side = 0 if by < 0 else 1
        if kind == 2:
            lines = pl.ds(0, rows if first < flat_count else rows + 2)
            source = terms.at[slots, :, lines, left if by < 0 else right]
            target = from_side.at[1 if by < 0 else 0, slots, :, lines]
        else:
            lines = pl.ds(0, rows) if kind == 0 else pl.ds(rows, 2)
            source = padded.at[slots, :, lines, 0 if by < 0 else columns - 1]
            target = padded.at[slots, :, lines, right if by < 0 else left]
        send = (col_send, corner_send, side_send)[kind]
        recv = (col_recv, corner_recv, side_recv)[kind]
        return remote(source, target, send.at[side, run], recv.at[side, run], "wa", wa + by)

    def start_columns(kind, run):
        for by in (-1, 1):

            @pl.when(exists["wa", by])
            def _(by=by):
                column_copy(kind, by, run).start()

    def columns_arrived(kind, run):
        for by in (-1, 1):

            @pl.when(exists["wa", -by])
            def _(by=by):
                column_copy(kind, by, run).wait_recv()

    chunk = queries // CHUNKS

    def x_copy(peer, part):
        tokens = pl.ds(part * chunk, chunk)
        return remote(
            x_ref.at[tokens],
            x_all.at[ha, tokens],
            x_send.at[peer, part],
            x_recv.at[ha, part],
            "ha",
            peer,
        )

    last = CHUNKS - 1

    def back_copy(pair):
        tokens = pl.ds(last * chunk, chunk)
        return remote(
            x_all.at[2 * pair + low, tokens],
            x_all.at[2 * pair + low, tokens],
            forward_send.at[pair, last],
            x_recv.at[2 * pair + low, last],
            "ha",
            partner,
        )

    def forward_copy(pair, part):
        tokens = pl.ds(part * chunk, chunk)
        return remote(
            x_all.at[partner, tokens],
            x_all.at[partner, tokens],
            forward_send.at[pair, part],
            x_recv.at[partner, part],
            "ha",
            2 * pair + low,
        )

    def x_landed(peer, part):
        tokens = pl.ds(part * chunk, chunk)
        landed(x_all.at[peer, tokens], x_recv.at[peer, part])

    def other_pairs(act):
        for pair in range(pairs):

            @pl.when(pair != high)
            def _(pair=pair):
                act(pair)

    for run in range(len(tall_runs)):
        start_rows(0, run)
    start_columns(0, 0)
    for part in range(CHUNKS):
        other_pairs(lambda pair: x_copy(2 * pair + low, part).start())

    query_id = lax.broadcasted_iota(jnp.int32, (1, queries), 1)
    key_id = lax.broadcasted_iota(jnp.int32, (code_ref.shape[0], 1), 0)
    query_frame = query_id // (rows * columns)
    query_row = (query_id // columns) % rows
    query_column = query_id % columns
    key_frame = key_id % frames
    key_row = key_id // (frames * (columns + 2))
    key_column = (key_id // frames) % (columns + 2)
    key_row = jnp.where(key_row == above, -1, jnp.where(key_row == below, rows, key_row))
    key_column = jnp.where(
        key_column == left, -1, jnp.where(key_column == right, columns, key_column)
    )
    outside = (
        (key_row + ha * rows < 0)
        | (key_row + ha * rows >= ha_count * rows)
        | (key_column + wa * columns < 0)
        | (key_column + wa * columns >= wa_count * columns)
    )
    key_row = jnp.where(outside, 1000, key_row)
    row_gap = jnp.abs(query_row - key_row)
    column_gap = jnp.abs(query_column - key_column)
    cells = jnp.zeros(code_ref.shape, jnp.int32)
    for row_reach in range(2):
        for column_reach in range(2):
            near = (row_gap <= row_reach) & (column_gap <= column_reach)
            cells = cells | jnp.where(near, 1 << (2 * row_reach + column_reach), 0)
    code = jnp.zeros(code_ref.shape, jnp.int32)
    for kind, (tile, frame_reach) in enumerate(FRAME_KINDS):
        gap = jnp.abs(query_frame // tile - key_frame // tile)
        code = code | jnp.where(gap <= frame_reach, cells << (4 * kind), 0)
    code_ref[...] = code
    for head in range(head_count):
        lanes = slice(head * head_size, (head + 1) * head_size)
        heads_q[head] = q_ref[:, lanes]
        heads_do[head] = do_ref[:, lanes]
    for run in range(1, len(runs)):
        start_columns(0, run)

    across = (((1,), (1,)), ((), ()))
    down = (((0,), (0,)), ((), ()))
    dot = functools.partial(lax.dot_general, preferred_element_type=jnp.float32)
    lift = scale * math.log2(math.e)

    def attend(run):
        first, size = runs[run]
        lines = rows if first < flat_count else rows + 2
        keys = lines * (columns + 2) * frames
        slots = range(first, first + size)
        q = [heads_q[order_ref[slot]] for slot in slots]
        do = [heads_do[order_ref[slot]] for slot in slots]
        k = [padded[slot, 0, :lines].reshape(keys, head_size) for slot in slots]
        v = [padded[slot, 1, :lines].reshape(keys, head_size) for slot in slots]
        bits = [jnp.left_shift(1, kind_ref[slot]) for slot in slots]
        each = range(size)
        scores = [dot(k[i], q[i], across) for i in each]
        upstream = [dot(v[i], do[i], across) for i in each]
        scores = [
            jnp.where((code_ref[:keys] & bits[i]) != 0, scores[i], HIDDEN) for i in each
        ]
        top = [jnp.max(scores[i], axis=0, keepdims=True) for i in each]
        lifted = [jnp.exp2((scores[i] - top[i]) * lift) for i in each]
        total = [jnp.sum(lifted[i], axis=0, keepdims=True) for i in each]
        weight = [(lifted[i] * (1.0 / total[i])).astype(bf) for i in each]
        wide = [weight[i].astype(jnp.float32) for i in each]
        delta = [jnp.sum(wide[i] * upstream[i], axis=0, keepdims=True) for i in each]
        slopes = [(wide[i] * (upstream[i] - delta[i])).astype(bf) for i in each]
        shape = (lines,) + terms.shape[3:]
        for i, slot in enumerate(slots):
            dv = jnp.dot(weight[i], do[i], preferred_element_type=jnp.float32)
            terms[slot, 1, :lines] = dv.astype(bf).reshape(shape)
            dk = jnp.dot(slopes[i], q[i], preferred_element_type=jnp.float32) * scale
            terms[slot, 0, :lines] = dk.astype(bf).reshape(shape)
            att_slots[slot] = dot(weight[i], v[i], down).astype(bf)
            dq_slots[slot] = (dot(slopes[i], k[i], down) * scale).astype(bf)

    tall_base = len(flat_runs)
    opened = 0

    def open_tall(run):
        relay(0, run)
        rows_arrived(0, run)
        start_columns(1, run)

    def pass_on(part):
        x_landed(partner, part)
        other_pairs(lambda pair: forward_copy(pair, part).start())

    passed = 0
    for run in range(len(runs)):
        columns_arrived(0, run)
        if run >= tall_base:
            while opened < min(run - tall_base + 2, len(tall_runs)):
                open_tall(opened)
                opened += 1
            columns_arrived(1, run - tall_base)
        attend(run)
        start_columns(2, run)
        if run < CHUNKS:
            x_copy(partner, run).start()
        if run < tall_base and opened < len(tall_runs):
            open_tall(opened)
            opened += 1
        if run >= 2 and passed < last:
            pass_on(passed)
            passed += 1
    for part in range(len(runs), CHUNKS):
        x_copy(partner, part).start()

    unit = slopes_own.shape[2]
    share = slopes_all.shape[1]
    pieces = head_size // unit
    for head in range(head_count):
        value = dq_slots[pos_ref[head]]
        for piece in range(pieces):
            slopes_own[head * pieces + piece] = value[:, piece * unit : (piece + 1) * unit]

    def slope_copy(peer):
        return remote(
            slopes_own.at[pl.ds(peer * share, share)],
            slopes_all.at[ha],
            slope_send.at[peer],
            slope_recv.at[ha],
            "ha",
            peer,
        )

    for peer in range(ha_count):

        @pl.when(peer != ha)
        def _(peer=peer):
            slope_copy(peer).start()

        @pl.when(peer == ha)
        def _(peer=peer):
            slopes_all[peer] = slopes_own[pl.ds(peer * share, share)]

    for part in range(passed, last):
        pass_on(part)

    def back(pair):
        x_landed(2 * pair + low, last)
        back_copy(pair).start()

    other_pairs(back)
    x_landed(partner, last)

    for head in range(head_count):
        att_ref[:, head * head_size : (head + 1) * head_size] = att_slots[pos_ref[head]]

    def fold_sides(run):
        first, size = runs[run]
        slots = pl.ds(first, size)
        lines = rows if first < flat_count else rows + 2
        columns_arrived(2, run)
        for side, line in ((0, 0), (1, columns - 1)):
            terms[slots, :, :lines, line] = (
                terms[slots, :, :lines, line] + from_side[side, slots, :, :lines]
            )

    for run in range(len(runs)):
        fold_sides(run)

    own_x.wait()
    for peer in range(ha_count):

        @pl.when(peer != ha)
        def _(peer=peer):
            landed(slopes_all.at[peer], slope_recv.at[peer])

    def wait_others(pair):
        for part in range(CHUNKS):
            if part < last:
                x_landed(2 * pair + low, part)
            x_landed(2 * pair + 1 - low, part)

    other_pairs(wait_others)

    core, chip = wa % 2, wa // 2
    chips = wa_count // 2
    halves = chips // 2
    parity, own_half = chip % 2, chip // 2
    block = x_all.shape[2] // chips
    tokens = ha_count * queries
    aligned = block % 128 == 0

    def core_copy(dest):
        return remote(
            product.at[dest, 1 - core],
            from_partner.at[dest],
            core_send.at[dest],
            core_recv.at[dest],
            "wa",
            wa + 1 - 2 * core,
        )

    def pair_copy(half):
        return remote(
            pair_sums.at[2 * half + 1 - parity],
            from_pair.at[half],
            pair_send.at[half],
            pair_recv.at[half],
            "wa",
            2 * (chip + 1 - 2 * parity) + core,
        )

    def chip_copy(half):
        return remote(
            chip_sums.at[half],
            from_chips.at[own_half],
            chip_send.at[half],
            chip_recv.at[own_half],
            "wa",
            2 * (2 * half + parity) + core,
        )

    others = [lax.rem(own_half + 1 + step, halves) for step in range(halves - 1)]
    columns_of = [slopes_all[:, at].reshape(tokens, unit) for at in range(share)]
    slope_block = columns_of[0] if share == 1 else jnp.concatenate(columns_of, axis=1)

    def form_product(dest):
        if aligned:
            lanes = pl.ds(pl.multiple_of(dest * block, block), block)
        else:
            lanes = slice(dest * block, (dest + 1) * block)
        value = dot(x_all[:, :, lanes].reshape(tokens, block), slope_block, down)
        product[dest] = value.astype(bf).reshape(product.shape[1:])
        core_copy(dest).start()

    def wide(value):
        return value.astype(jnp.float32)

    def core_sum(dest):
        core_copy(dest).wait_recv()
        pair_sums[dest] = (wide(product[dest, core]) + wide(from_partner[dest])).astype(bf)

    def chip_sum(half):
        pair_copy(half).wait_recv()
        total = wide(pair_sums[2 * half + parity]) + wide(from_pair[half])
        chip_sums[half] = total.astype(bf)

    if aligned:
        for half in others + [own_half]:
            form_product(2 * half + 1 - parity)
            form_product(2 * half + parity)
    else:
        for dest in range(chips):
            form_product(dest)
    for half in others:
        core_sum(2 * half + 1 - parity)
        pair_copy(half).start()
        core_sum(2 * half + parity)
    for run in range(len(tall_runs)):
        start_rows(1, run)
    for half in others:
        chip_sum(half)
        chip_copy(half).start()
    core_sum(2 * own_half + 1 - parity)
    pair_copy(own_half).start()
    core_sum(2 * own_half + parity)
    for run in range(len(tall_runs)):
        relay(1, run)
    chip_sum(own_half)
    from_chips[own_half] = chip_sums[own_half]

    for run in range(len(tall_runs)):
        rows_arrived(1, run)
        first, size = tall_runs[run]
        slots = pl.ds(first, size)
        near = pl.ds(first - flat_count, size)
        for side, line in ((0, 0), (1, rows - 1)):
            terms[slots, :, line, :columns] = (
                terms[slots, :, line, :columns] + from_row[side, near]
            )

    for head in range(head_count):
        here = slice(head * head_size, (head + 1) * head_size)
        dk_ref[:, :, :, here] = terms[pos_ref[head], 0, :rows, :columns]
        dv_ref[:, :, :, here] = terms[pos_ref[head], 1, :rows, :columns]

    for half in others:
        landed(from_chips.at[half], chip_recv.at[half])
    gathered = from_chips[0].astype(jnp.float32)
    for half in range(1, halves):
        gathered = gathered + from_chips[half].astype(jnp.float32)
    tokens_all = queries * ha_count * wa_count
    weight_ref[...] = (gathered * (1.0 / math.sqrt(tokens_all))).astype(weight_ref.dtype)

    for kind in range(2):
        for run in range(len(tall_runs)):
            each_row_copy(kind, run, lambda copy: copy.wait_send())
            if relayed:
                for at, by in ((0, -1), (ha_count - 1, 1)):

                    @pl.when(ha == at)
                    def _(by=by, kind=kind, run=run):
                        relay_copy(kind, by, run).wait_send()

    for kind, count in ((0, len(runs)), (1, len(tall_runs)), (2, len(runs))):
        for run in range(count):
            for by in (-1, 1):

                @pl.when(exists["wa", by])
                def _(by=by, kind=kind, run=run):
                    column_copy(kind, by, run).wait_send()

    def x_sent(pair):
        for part in range(CHUNKS):
            x_copy(2 * pair + low, part).wait_send()
            (forward_copy(pair, part) if part < last else back_copy(pair)).wait_send()

    for part in range(CHUNKS):
        x_copy(partner, part).wait_send()
    other_pairs(x_sent)
    for peer in range(ha_count):

        @pl.when(peer != ha)
        def _(peer=peer):
            slope_copy(peer).wait_send()

    for dest in range(chips):
        core_copy(dest).wait_send()
    for half in range(halves):
        pair_copy(half).wait_send()
    for half in others:
        chip_copy(half).wait_send()


def on_device(
    which, inputs, query_vectors, key_vectors, value_vectors, output_cotangent, window
):
    tall_count = TALLS[which]
    frames, rows, columns, feature = query_vectors.shape
    head_count = window.shape[0]
    head_size = feature // head_count
    queries = frames * rows * columns
    bf = jnp.bfloat16

    def tokens(x):
        return x.reshape(queries, x.shape[3])

    def cells(x):
        return x.transpose(1, 2, 0, 3)

    ha_count, wa_count = lax.axis_size("ha"), lax.axis_size("wa")
    chips = wa_count // 2
    halves = chips // 2
    slice_rows = inputs.shape[3] // wa_count
    slice_columns = feature // ha_count
    unit = math.gcd(head_size, slice_columns)
    cell = (frames, head_size)
    tall = (head_count, 2, rows + 2, columns + 2) + cell
    keys = (rows + 2) * (columns + 2) * frames
    part = (slice_rows, slice_columns)
    tall_runs = len(split(head_count - tall_count, head_count))
    runs = len(split(0, head_count - tall_count)) + tall_runs
    vmem = pl.BlockSpec(memory_space=pltpu.VMEM)
    dma = pltpu.SemaphoreType.DMA
    buffers = [
        pltpu.VMEM((keys, queries), jnp.int32),
        pltpu.VMEM((head_count, 2, rows, columns) + cell, bf),
        pltpu.VMEM((head_count, queries, head_size), bf),
        pltpu.VMEM((head_count, queries, head_size), bf),
        pltpu.VMEM(tall, bf),
        pltpu.VMEM(tall, bf),
        pltpu.VMEM((head_count, queries, head_size), bf),
        pltpu.VMEM((head_count, queries, head_size), bf),
        pltpu.VMEM((2, head_count, 2, rows + 2) + cell, bf),
        pltpu.VMEM((2, tall_count, 2, columns) + cell, bf),
        pltpu.VMEM((tall_count, columns) + cell, bf),
        pltpu.VMEM((tall_count, columns) + cell, bf),
        pltpu.VMEM((feature // unit, queries, unit), bf),
        pltpu.VMEM((ha_count, queries, inputs.shape[3]), bf),
        pltpu.VMEM((ha_count, slice_columns // unit, queries, unit), bf),
        pltpu.VMEM((chips, 2) + part, bf),
        pltpu.VMEM((chips,) + part, bf),
        pltpu.VMEM((chips,) + part, bf),
        pltpu.VMEM((halves,) + part, bf),
        pltpu.VMEM((halves,) + part, bf),
        pltpu.VMEM((halves,) + part, bf),
    ]
    held = sum(
        math.prod(buffer.shape) * jnp.dtype(buffer.dtype).itemsize for buffer in buffers
    )
    held += 10 * queries * feature * 2
    att, dk, dv, weight_gradient = pl.pallas_call(
        functools.partial(attention_kernel, tall_count),
        out_shape=(
            jax.ShapeDtypeStruct((queries, feature), bf),
            jax.ShapeDtypeStruct((rows, columns, frames, feature), bf),
            jax.ShapeDtypeStruct((rows, columns, frames, feature), bf),
            jax.ShapeDtypeStruct(part, bf),
        ),
        in_specs=[pl.BlockSpec(memory_space=pltpu.SMEM), vmem, vmem, vmem, vmem, vmem],
        out_specs=(vmem, vmem, vmem, vmem),
        scratch_shapes=[
            pltpu.SMEM((head_count,), jnp.int32),
            pltpu.SMEM((head_count,), jnp.int32),
            pltpu.SMEM((head_count,), jnp.int32),
            *buffers,
            dma((1,)),
            dma((2, 2, 2, tall_runs)),
            dma((2, 2, 2, tall_runs)),
            dma((2, tall_runs)),
            dma((2, tall_runs)),
            dma((2, runs)),
            dma((2, runs)),
            dma((2, tall_runs)),
            dma((2, tall_runs)),
            dma((2, runs)),
            dma((2, runs)),
            dma((ha_count, CHUNKS)),
            dma((ha_count, CHUNKS)),
            dma((ha_count // 2, CHUNKS)),
            dma((ha_count,)),
            dma((ha_count,)),
            dma((chips,)),
            dma((chips,)),
            dma((halves,)),
            dma((halves,)),
            dma((halves,)),
            dma((halves,)),
        ],
        compiler_params=pltpu.CompilerParams(
            collective_id=which, has_side_effects=True, vmem_limit_bytes=held + 4 * 1024 * 1024
        ),
    )(
        window.T,
        tokens(query_vectors),
        tokens(output_cotangent),
        cells(key_vectors),
        cells(value_vectors),
        tokens(inputs),
    )

    def to_grid(x):
        return x.transpose(2, 0, 1, 3)

    return (att.reshape(query_vectors.shape), to_grid(dk), to_grid(dv), weight_gradient)


def by_reach(*args):
    reaching = jnp.sum(args[5][:, 2])
    which = sum((reaching > most).astype(jnp.int32) for most in TALLS[:-1])
    branches = [functools.partial(on_device, at) for at in range(len(TALLS))]
    return lax.switch(which, branches, *args)


def solution(mesh):
    cells = P(None, "ha", "wa", None)
    return jax.shard_map(
        by_reach,
        mesh=mesh,
        in_specs=(cells, cells, cells, cells, cells, P()),
        out_specs=(cells, cells, cells, P("wa", "ha")),
        check_vma=False,
    )
```

```python
import functools
import math

import jax
import jax.numpy as jnp
from jax import lax
from jax.experimental import pallas as pl
from jax.experimental.pallas import tpu as pltpu
from jax.sharding import PartitionSpec as P

MESH = pl.DeviceIdType.MESH
TALLS = (6, 8, 12)
BATCH = 3
CHUNKS = 4
HIDDEN = -1e30
FRAME_KINDS = ((1, 0), (1, 1), (1, 2), (2, 0), (2, 1))


def split(low, high):
    count = high - low
    runs = -(-count // BATCH)
    out = []
    for at in range(runs):
        size = count // runs + (1 if at < count % runs else 0)
        out.append((low, size))
        low += size
    return out


def attention_kernel(
    tall_count,
    window_ref,
    q_ref,
    do_ref,
    k_ref,
    v_ref,
    x_ref,
    att_ref,
    dk_ref,
    dv_ref,
    weight_ref,
    order_ref,
    pos_ref,
    kind_ref,
    code_ref,
    heads_kv,
    heads_q,
    heads_do,
    padded,
    terms,
    att_slots,
    dq_slots,
    from_side,
    from_row,
    relay_rows,
    relay_terms,
    slopes_own,
    x_all,
    slopes_all,
    product,
    from_partner,
    pair_sums,
    from_pair,
    chip_sums,
    from_chips,
    row_send,
    row_recv,
    relay_send,
    relay_recv,
    col_send,
    col_recv,
    corner_send,
    corner_recv,
    side_send,
    side_recv,
    x_send,
    x_recv,
    forward_send,
    slope_send,
    slope_recv,
    core_send,
    core_recv,
    pair_send,
    pair_recv,
    chip_send,
    chip_recv,
):
    rows, columns, frames, _ = k_ref.shape
    head_count = padded.shape[0]
    head_size = padded.shape[-1]
    queries = rows * columns * frames
    bf = jnp.bfloat16
    scale = 1.0 / math.sqrt(head_size)
    ha_count, wa_count = lax.axis_size("ha"), lax.axis_size("wa")
    ha, wa = lax.axis_index("ha"), lax.axis_index("wa")
    flat_count = head_count - tall_count
    flat_runs = split(0, flat_count)
    tall_runs = split(flat_count, head_count)
    runs = flat_runs + tall_runs
    place = {"ha": ha, "wa": wa}
    exists = {
        ("ha", -1): ha > 0,
        ("ha", 1): ha < ha_count - 1,
        ("wa", -1): wa > 0,
        ("wa", 1): wa < wa_count - 1,
    }
    above, below = rows, rows + 1
    left, right = columns, columns + 1
    low, high = ha % 2, ha // 2
    partner = 2 * high + 1 - low
    pairs = ha_count // 2
    relayed = pairs == 2

    tall_slots = pl.ds(flat_count, tall_count)
    for at, side, line in ((0, 0, above), (ha_count - 1, 1, below)):

        @pl.when(ha == at)
        def _(side=side, line=line):
            hidden = padded.at[tall_slots, :, line]
            hidden[...] = jnp.zeros(hidden.shape, bf)
            from_row[side] = jnp.zeros(from_row.shape[1:], bf)

    for at, side, line in ((0, 0, left), (wa_count - 1, 1, right)):

        @pl.when(wa == at)
        def _(side=side, line=line):
            for count, first, lines in (
                (flat_count, 0, rows),
                (tall_count, flat_count, rows + 2),
            ):
                if count:
                    hidden = padded.at[pl.ds(first, count), :, pl.ds(0, lines), line]
                    hidden[...] = jnp.zeros(hidden.shape, bf)
                    fold = from_side.at[side, pl.ds(first, count), :, pl.ds(0, lines)]
                    fold[...] = jnp.zeros(fold.shape, bf)

    barrier = pltpu.get_barrier_semaphore()
    for axis, count in (("ha", ha_count), ("wa", wa_count)):
        for step in range(1, count):
            pl.semaphore_signal(
                barrier,
                inc=1,
                device_id={axis: (place[axis] + step) % count},
                device_id_type=MESH,
            )

    reach = [window_ref[2, head] for head in range(head_count)]
    next_tall = head_count - sum(reach)
    next_flat = 0
    spots = []
    for head in range(head_count):
        spot = jnp.where(reach[head] > 0, next_tall, next_flat)
        next_tall = next_tall + reach[head]
        next_flat = next_flat + 1 - reach[head]
        pos_ref[head] = spot
        spots.append(spot)
    kinds = []
    for head in range(head_count):
        tile = jnp.where(window_ref[0, head] == 2, 3, 0) + window_ref[1, head]
        kinds.append(4 * tile + 2 * reach[head] + window_ref[3, head])
    for slot in range(head_count):
        here = [spots[head] == slot for head in range(head_count)]
        order_ref[slot] = sum(jnp.where(here[head], head, 0) for head in range(head_count))
        kind_ref[slot] = sum(jnp.where(here[head], kinds[head], 0) for head in range(head_count))

    for head in range(head_count):
        lanes = slice(head * head_size, (head + 1) * head_size)
        heads_kv[head, 0] = k_ref[:, :, :, lanes]
        heads_kv[head, 1] = v_ref[:, :, :, lanes]
    for slot in range(head_count):
        padded[slot, :, :rows, :columns] = heads_kv[order_ref[slot]]

    pl.semaphore_wait(barrier, ha_count + wa_count - 2)

    def remote(source, target, send, recv, axis, device):
        return pltpu.make_async_remote_copy(
            src_ref=source,
            dst_ref=target,
            send_sem=send,
            recv_sem=recv,
            device_id={axis: device},
            device_id_type=MESH,
        )

    def landed(buffer, sem):
        pltpu.make_async_copy(buffer, buffer, sem).wait()

    def detour(by):
        if not relayed:
            return None
        return ha == (1 if by > 0 else pairs)

    def row_source(kind, by, part, run):
        first, size = tall_runs[run]
        if kind == 0:
            return padded.at[
                pl.ds(first, size), part, 0 if by < 0 else rows - 1, pl.ds(0, columns)
            ]
        return terms.at[
            pl.ds(first, size), part, above if by < 0 else below, pl.ds(0, columns)
        ]

    def row_target(kind, by, part, run):
        first, size = tall_runs[run]
        if kind == 0:
            return padded.at[
                pl.ds(first, size), part, below if by < 0 else above, pl.ds(0, columns)
            ]
        return from_row.at[1 if by < 0 else 0, pl.ds(first - flat_count, size), part]

    def relay_buffer(kind, run):
        first, size = tall_runs[run]
        return (relay_rows, relay_terms)[kind].at[pl.ds(first - flat_count, size)]

    def row_copy(kind, by, part, run):
        side = 0 if by < 0 else 1
        return remote(
            row_source(kind, by, part, run),
            row_target(kind, by, part, run),
            row_send.at[kind, side, part, run],
            row_recv.at[kind, side, part, run],
            "ha",
            ha + by,
        )

    def detour_copy(kind, by, run):
        side = 0 if by < 0 else 1
        return remote(
            row_source(kind, by, 1, run),
            relay_buffer(kind, run),
            row_send.at[kind, side, 1, run],
            relay_recv.at[kind, run],
            "ha",
            (ha + 2) % ha_count,
        )

    def relay_copy(kind, by, run):
        side = 0 if by < 0 else 1
        return remote(
            relay_buffer(kind, run),
            row_target(kind, by, 1, run),
            relay_send.at[kind, run],
            row_recv.at[kind, side, 1, run],
            "ha",
            partner,
        )

    def each_row_copy(kind, run, act):
        for by in (-1, 1):
            turn = detour(by)
            for part in range(2):
                direct = exists["ha", by]
                if part == 1 and turn is not None:
                    direct = direct & jnp.logical_not(turn)

                    @pl.when(turn)
                    def _(by=by):
                        act(detour_copy(kind, by, run))

                @pl.when(direct)
                def _(by=by, part=part):
                    act(row_copy(kind, by, part, run))

    def start_rows(kind, run):
        each_row_copy(kind, run, lambda copy: copy.start())

    def relay(kind, run):
        if relayed:
            for at, by in ((0, -1), (ha_count - 1, 1)):

                @pl.when(ha == at)
                def _(by=by):
                    landed(relay_buffer(kind, run), relay_recv.at[kind, run])
                    relay_copy(kind, by, run).start()

    def rows_arrived(kind, run):
        for by in (-1, 1):

            @pl.when(exists["ha", -by])
            def _(by=by):
                for part in range(2):
                    row_copy(kind, by, part, run).wait_recv()

    def column_copy(kind, by, run):
        first, size = (tall_runs if kind == 1 else runs)[run]
        slots = pl.ds(first, size)
        side = 0 if by < 0 else 1
        if kind == 2:
            lines = pl.ds(0, rows if first < flat_count else rows + 2)
            source = terms.at[slots, :, lines, left if by < 0 else right]
            target = from_side.at[1 if by < 0 else 0, slots, :, lines]
        else:
            lines = pl.ds(0, rows) if kind == 0 else pl.ds(rows, 2)
            source = padded.at[slots, :, lines, 0 if by < 0 else columns - 1]
            target = padded.at[slots, :, lines, right if by < 0 else left]
        send = (col_send, corner_send, side_send)[kind]
        recv = (col_recv, corner_recv, side_recv)[kind]
        return remote(source, target, send.at[side, run], recv.at[side, run], "wa", wa + by)

    def start_columns(kind, run):
        for by in (-1, 1):

            @pl.when(exists["wa", by])
            def _(by=by):
                column_copy(kind, by, run).start()

    def columns_arrived(kind, run):
        for by in (-1, 1):

            @pl.when(exists["wa", -by])
            def _(by=by):
                column_copy(kind, by, run).wait_recv()

    chunk = queries // CHUNKS

    def x_copy(peer, part):
        tokens = pl.ds(part * chunk, chunk)
        return remote(
            x_all.at[ha, tokens],
            x_all.at[ha, tokens],
            x_send.at[peer, part],
            x_recv.at[ha, part],
            "ha",
            peer,
        )

    last = CHUNKS - 1

    def back_copy(pair):
        tokens = pl.ds(last * chunk, chunk)
        return remote(
            x_all.at[2 * pair + low, tokens],
            x_all.at[2 * pair + low, tokens],
            forward_send.at[pair, last],
            x_recv.at[2 * pair + low, last],
            "ha",
            partner,
        )

    def forward_copy(pair, part):
        tokens = pl.ds(part * chunk, chunk)
        return remote(
            x_all.at[partner, tokens],
            x_all.at[partner, tokens],
            forward_send.at[pair, part],
            x_recv.at[partner, part],
            "ha",
            2 * pair + low,
        )

    def x_landed(peer, part):
        tokens = pl.ds(part * chunk, chunk)
        landed(x_all.at[peer, tokens], x_recv.at[peer, part])

    def other_pairs(act):
        for pair in range(pairs):

            @pl.when(pair != high)
            def _(pair=pair):
                act(pair)

    for run in range(len(tall_runs)):
        start_rows(0, run)
    start_columns(0, 0)
    for at in range(x_ref.shape[3] // head_size):
        lanes = slice(at * head_size, (at + 1) * head_size)
        x_all[ha, :, lanes] = x_ref[:, :, :, lanes].reshape(queries, head_size)
    for run in range(1, len(runs)):
        start_columns(0, run)
    for part in range(CHUNKS):
        other_pairs(lambda pair: x_copy(2 * pair + low, part).start())

    query_id = lax.broadcasted_iota(jnp.int32, (1, queries), 1)
    key_id = lax.broadcasted_iota(jnp.int32, (code_ref.shape[0], 1), 0)
    query_frame = query_id // (rows * columns)
    query_row = (query_id // columns) % rows
    query_column = query_id % columns
    key_frame = key_id % frames
    key_row = key_id // (frames * (columns + 2))
    key_column = (key_id // frames) % (columns + 2)
    key_row = jnp.where(key_row == above, -1, jnp.where(key_row == below, rows, key_row))
    key_column = jnp.where(
        key_column == left, -1, jnp.where(key_column == right, columns, key_column)
    )
    outside = (
        (key_row + ha * rows < 0)
        | (key_row + ha * rows >= ha_count * rows)
        | (key_column + wa * columns < 0)
        | (key_column + wa * columns >= wa_count * columns)
    )
    key_row = jnp.where(outside, 1000, key_row)
    row_gap = jnp.abs(query_row - key_row)
    column_gap = jnp.abs(query_column - key_column)
    cells = jnp.zeros(code_ref.shape, jnp.int32)
    for row_reach in range(2):
        for column_reach in range(2):
            near = (row_gap <= row_reach) & (column_gap <= column_reach)
            cells = cells | jnp.where(near, 1 << (2 * row_reach + column_reach), 0)
    code = jnp.zeros(code_ref.shape, jnp.int32)
    for kind, (tile, frame_reach) in enumerate(FRAME_KINDS):
        gap = jnp.abs(query_frame // tile - key_frame // tile)
        code = code | jnp.where(gap <= frame_reach, cells << (4 * kind), 0)
    code_ref[...] = code
    for head in range(head_count):
        lanes = slice(head * head_size, (head + 1) * head_size)
        heads_q[head] = q_ref[:, :, :, lanes].reshape(queries, head_size)
        heads_do[head] = do_ref[:, :, :, lanes].reshape(queries, head_size)

    across = (((1,), (1,)), ((), ()))
    down = (((0,), (0,)), ((), ()))
    dot = functools.partial(lax.dot_general, preferred_element_type=jnp.float32)
    lift = scale * math.log2(math.e)

    def attend(run):
        first, size = runs[run]
        lines = rows if first < flat_count else rows + 2
        keys = lines * (columns + 2) * frames
        slots = range(first, first + size)
        q = [heads_q[order_ref[slot]] for slot in slots]
        do = [heads_do[order_ref[slot]] for slot in slots]
        k = [padded[slot, 0, :lines].reshape(keys, head_size) for slot in slots]
        v = [padded[slot, 1, :lines].reshape(keys, head_size) for slot in slots]
        bits = [jnp.left_shift(1, kind_ref[slot]) for slot in slots]
        each = range(size)
        scores = [dot(k[i], q[i], across) for i in each]
        upstream = [dot(v[i], do[i], across) for i in each]
        scores = [
            jnp.where((code_ref[:keys] & bits[i]) != 0, scores[i], HIDDEN) for i in each
        ]
        top = [jnp.max(scores[i], axis=0, keepdims=True) for i in each]
        lifted = [jnp.exp2((scores[i] - top[i]) * lift) for i in each]
        total = [jnp.sum(lifted[i], axis=0, keepdims=True) for i in each]
        weight = [(lifted[i] * (1.0 / total[i])).astype(bf) for i in each]
        wide = [weight[i].astype(jnp.float32) for i in each]
        delta = [jnp.sum(wide[i] * upstream[i], axis=0, keepdims=True) for i in each]
        slopes = [(wide[i] * (upstream[i] - delta[i])).astype(bf) for i in each]
        shape = (lines,) + terms.shape[3:]
        for i, slot in enumerate(slots):
            dv = jnp.dot(weight[i], do[i], preferred_element_type=jnp.float32)
            terms[slot, 1, :lines] = dv.astype(bf).reshape(shape)
            dk = jnp.dot(slopes[i], q[i], preferred_element_type=jnp.float32) * scale
            terms[slot, 0, :lines] = dk.astype(bf).reshape(shape)
            att_slots[slot] = dot(weight[i], v[i], down).astype(bf)
            dq_slots[slot] = (dot(slopes[i], k[i], down) * scale).astype(bf)

    tall_base = len(flat_runs)
    opened = 0

    def open_tall(run):
        relay(0, run)
        rows_arrived(0, run)
        start_columns(1, run)

    def pass_on(part):
        x_landed(partner, part)
        other_pairs(lambda pair: forward_copy(pair, part).start())

    passed = 0
    for run in range(len(runs)):
        columns_arrived(0, run)
        if run >= tall_base:
            while opened < min(run - tall_base + 2, len(tall_runs)):
                open_tall(opened)
                opened += 1
            columns_arrived(1, run - tall_base)
        attend(run)
        start_columns(2, run)
        if run < CHUNKS:
            x_copy(partner, run).start()
        if run < tall_base and opened < len(tall_runs):
            open_tall(opened)
            opened += 1
        if run >= 2 and passed < last:
            pass_on(passed)
            passed += 1
    for part in range(len(runs), CHUNKS):
        x_copy(partner, part).start()

    unit = slopes_own.shape[2]
    share = slopes_all.shape[1]
    pieces = head_size // unit
    for head in range(head_count):
        value = dq_slots[pos_ref[head]]
        for piece in range(pieces):
            slopes_own[head * pieces + piece] = value[:, piece * unit : (piece + 1) * unit]

    def slope_copy(peer):
        return remote(
            slopes_own.at[pl.ds(peer * share, share)],
            slopes_all.at[ha],
            slope_send.at[peer],
            slope_recv.at[ha],
            "ha",
            peer,
        )

    for peer in range(ha_count):

        @pl.when(peer != ha)
        def _(peer=peer):
            slope_copy(peer).start()

        @pl.when(peer == ha)
        def _(peer=peer):
            slopes_all[peer] = slopes_own[pl.ds(peer * share, share)]

    for part in range(passed, last):
        pass_on(part)

    def back(pair):
        x_landed(2 * pair + low, last)
        back_copy(pair).start()

    other_pairs(back)
    x_landed(partner, last)

    for head in range(head_count):
        att_ref[:, head * head_size : (head + 1) * head_size] = att_slots[pos_ref[head]]

    def fold_sides(run):
        first, size = runs[run]
        slots = pl.ds(first, size)
        lines = rows if first < flat_count else rows + 2
        columns_arrived(2, run)
        for side, line in ((0, 0), (1, columns - 1)):
            terms[slots, :, :lines, line] = (
                terms[slots, :, :lines, line] + from_side[side, slots, :, :lines]
            )

    for run in range(len(runs)):
        fold_sides(run)

    for peer in range(ha_count):

        @pl.when(peer != ha)
        def _(peer=peer):
            landed(slopes_all.at[peer], slope_recv.at[peer])

    def wait_others(pair):
        for part in range(CHUNKS):
            if part < last:
                x_landed(2 * pair + low, part)
            x_landed(2 * pair + 1 - low, part)

    other_pairs(wait_others)

    core, chip = wa % 2, wa // 2
    chips = wa_count // 2
    halves = chips // 2
    parity, own_half = chip % 2, chip // 2
    block = x_all.shape[2] // chips
    tokens = ha_count * queries
    aligned = block % 128 == 0

    def core_copy(dest):
        return remote(
            product.at[dest, 1 - core],
            from_partner.at[dest],
            core_send.at[dest],
            core_recv.at[dest],
            "wa",
            wa + 1 - 2 * core,
        )

    def pair_copy(half):
        return remote(
            pair_sums.at[2 * half + 1 - parity],
            from_pair.at[half],
            pair_send.at[half],
            pair_recv.at[half],
            "wa",
            2 * (chip + 1 - 2 * parity) + core,
        )

    def chip_copy(half):
        return remote(
            chip_sums.at[half],
            from_chips.at[own_half],
            chip_send.at[half],
            chip_recv.at[own_half],
            "wa",
            2 * (2 * half + parity) + core,
        )

    others = [lax.rem(own_half + 1 + step, halves) for step in range(halves - 1)]
    columns_of = [slopes_all[:, at].reshape(tokens, unit) for at in range(share)]
    slope_block = columns_of[0] if share == 1 else jnp.concatenate(columns_of, axis=1)

    def form_product(dest):
        if aligned:
            lanes = pl.ds(pl.multiple_of(dest * block, block), block)
        else:
            lanes = slice(dest * block, (dest + 1) * block)
        value = dot(x_all[:, :, lanes].reshape(tokens, block), slope_block, down)
        product[dest] = value.astype(bf).reshape(product.shape[1:])
        core_copy(dest).start()

    def wide(value):
        return value.astype(jnp.float32)

    def core_sum(dest):
        core_copy(dest).wait_recv()
        pair_sums[dest] = (wide(product[dest, core]) + wide(from_partner[dest])).astype(bf)

    def chip_sum(half):
        pair_copy(half).wait_recv()
        total = wide(pair_sums[2 * half + parity]) + wide(from_pair[half])
        chip_sums[half] = total.astype(bf)

    if aligned:
        for half in others + [own_half]:
            form_product(2 * half + 1 - parity)
            form_product(2 * half + parity)
    else:
        for dest in range(chips):
            form_product(dest)
    for half in others:
        core_sum(2 * half + 1 - parity)
        pair_copy(half).start()
        core_sum(2 * half + parity)
    for run in range(len(tall_runs)):
        start_rows(1, run)
    for half in others:
        chip_sum(half)
        chip_copy(half).start()
    core_sum(2 * own_half + 1 - parity)
    pair_copy(own_half).start()
    core_sum(2 * own_half + parity)
    for run in range(len(tall_runs)):
        relay(1, run)
    chip_sum(own_half)
    from_chips[own_half] = chip_sums[own_half]

    for run in range(len(tall_runs)):
        rows_arrived(1, run)
        first, size = tall_runs[run]
        slots = pl.ds(first, size)
        near = pl.ds(first - flat_count, size)
        for side, line in ((0, 0), (1, rows - 1)):
            terms[slots, :, line, :columns] = (
                terms[slots, :, line, :columns] + from_row[side, near]
            )

    for head in range(head_count):
        here = slice(head * head_size, (head + 1) * head_size)
        dk_ref[:, :, :, here] = terms[pos_ref[head], 0, :rows, :columns]
        dv_ref[:, :, :, here] = terms[pos_ref[head], 1, :rows, :columns]

    for half in others:
        landed(from_chips.at[half], chip_recv.at[half])
    gathered = from_chips[0].astype(jnp.float32)
    for half in range(1, halves):
        gathered = gathered + from_chips[half].astype(jnp.float32)
    weight_ref[...] = gathered

    for kind in range(2):
        for run in range(len(tall_runs)):
            each_row_copy(kind, run, lambda copy: copy.wait_send())
            if relayed:
                for at, by in ((0, -1), (ha_count - 1, 1)):

                    @pl.when(ha == at)
                    def _(by=by, kind=kind, run=run):
                        relay_copy(kind, by, run).wait_send()

    for kind, count in ((0, len(runs)), (1, len(tall_runs)), (2, len(runs))):
        for run in range(count):
            for by in (-1, 1):

                @pl.when(exists["wa", by])
                def _(by=by, kind=kind, run=run):
                    column_copy(kind, by, run).wait_send()

    def x_sent(pair):
        for part in range(CHUNKS):
            x_copy(2 * pair + low, part).wait_send()
            (forward_copy(pair, part) if part < last else back_copy(pair)).wait_send()

    for part in range(CHUNKS):
        x_copy(partner, part).wait_send()
    other_pairs(x_sent)
    for peer in range(ha_count):

        @pl.when(peer != ha)
        def _(peer=peer):
            slope_copy(peer).wait_send()

    for dest in range(chips):
        core_copy(dest).wait_send()
    for half in range(halves):
        pair_copy(half).wait_send()
    for half in others:
        chip_copy(half).wait_send()


def on_device(
    which, inputs, query_vectors, key_vectors, value_vectors, output_cotangent, window
):
    tall_count = TALLS[which]
    frames, rows, columns, feature = query_vectors.shape
    head_count = window.shape[0]
    head_size = feature // head_count
    queries = frames * rows * columns
    bf = jnp.bfloat16

    def cells(x):
        return x.transpose(1, 2, 0, 3)

    ha_count, wa_count = lax.axis_size("ha"), lax.axis_size("wa")
    chips = wa_count // 2
    halves = chips // 2
    slice_rows = inputs.shape[3] // wa_count
    slice_columns = feature // ha_count
    unit = math.gcd(head_size, slice_columns)
    cell = (frames, head_size)
    tall = (head_count, 2, rows + 2, columns + 2) + cell
    keys = (rows + 2) * (columns + 2) * frames
    part = (slice_rows, slice_columns)
    tall_runs = len(split(head_count - tall_count, head_count))
    runs = len(split(0, head_count - tall_count)) + tall_runs
    vmem = pl.BlockSpec(memory_space=pltpu.VMEM)
    dma = pltpu.SemaphoreType.DMA
    buffers = [
        pltpu.VMEM((keys, queries), jnp.int32),
        pltpu.VMEM((head_count, 2, rows, columns) + cell, bf),
        pltpu.VMEM((head_count, queries, head_size), bf),
        pltpu.VMEM((head_count, queries, head_size), bf),
        pltpu.VMEM(tall, bf),
        pltpu.VMEM(tall, bf),
        pltpu.VMEM((head_count, queries, head_size), bf),
        pltpu.VMEM((head_count, queries, head_size), bf),
        pltpu.VMEM((2, head_count, 2, rows + 2) + cell, bf),
        pltpu.VMEM((2, tall_count, 2, columns) + cell, bf),
        pltpu.VMEM((tall_count, columns) + cell, bf),
        pltpu.VMEM((tall_count, columns) + cell, bf),
        pltpu.VMEM((feature // unit, queries, unit), bf),
        pltpu.VMEM((ha_count, queries, inputs.shape[3]), bf),
        pltpu.VMEM((ha_count, slice_columns // unit, queries, unit), bf),
        pltpu.VMEM((chips, 2) + part, bf),
        pltpu.VMEM((chips,) + part, bf),
        pltpu.VMEM((chips,) + part, bf),
        pltpu.VMEM((halves,) + part, bf),
        pltpu.VMEM((halves,) + part, bf),
        pltpu.VMEM((halves,) + part, bf),
    ]
    held = sum(
        math.prod(buffer.shape) * jnp.dtype(buffer.dtype).itemsize for buffer in buffers
    )
    held += 10 * queries * feature * 2
    att, dk, dv, weight_gradient = pl.pallas_call(
        functools.partial(attention_kernel, tall_count),
        out_shape=(
            jax.ShapeDtypeStruct((queries, feature), bf),
            jax.ShapeDtypeStruct((rows, columns, frames, feature), bf),
            jax.ShapeDtypeStruct((rows, columns, frames, feature), bf),
            jax.ShapeDtypeStruct(part, jnp.float32),
        ),
        in_specs=[pl.BlockSpec(memory_space=pltpu.SMEM), vmem, vmem, vmem, vmem, vmem],
        out_specs=(vmem, vmem, vmem, vmem),
        scratch_shapes=[
            pltpu.SMEM((head_count,), jnp.int32),
            pltpu.SMEM((head_count,), jnp.int32),
            pltpu.SMEM((head_count,), jnp.int32),
            *buffers,
            dma((2, 2, 2, tall_runs)),
            dma((2, 2, 2, tall_runs)),
            dma((2, tall_runs)),
            dma((2, tall_runs)),
            dma((2, runs)),
            dma((2, runs)),
            dma((2, tall_runs)),
            dma((2, tall_runs)),
            dma((2, runs)),
            dma((2, runs)),
            dma((ha_count, CHUNKS)),
            dma((ha_count, CHUNKS)),
            dma((ha_count // 2, CHUNKS)),
            dma((ha_count,)),
            dma((ha_count,)),
            dma((chips,)),
            dma((chips,)),
            dma((halves,)),
            dma((halves,)),
            dma((halves,)),
            dma((halves,)),
        ],
        compiler_params=pltpu.CompilerParams(
            collective_id=which, has_side_effects=True, vmem_limit_bytes=held + 2 * 1024 * 1024
        ),
    )(
        window.T,
        query_vectors,
        output_cotangent,
        cells(key_vectors),
        cells(value_vectors),
        inputs,
    )

    tokens_all = queries * ha_count * wa_count
    weight_gradient = (weight_gradient * (1.0 / math.sqrt(tokens_all))).astype(bf)

    def to_grid(x):
        return x.transpose(2, 0, 1, 3)

    return (att.reshape(query_vectors.shape), to_grid(dk), to_grid(dv), weight_gradient)


def by_reach(*args):
    reaching = jnp.sum(args[5][:, 2])
    which = sum((reaching > most).astype(jnp.int32) for most in TALLS[:-1])
    branches = [functools.partial(on_device, at) for at in range(len(TALLS))]
    return lax.switch(which, branches, *args)


def solution(mesh):
    cells = P(None, "ha", "wa", None)
    return jax.shard_map(
        by_reach,
        mesh=mesh,
        in_specs=(cells, cells, cells, cells, cells, P()),
        out_specs=(cells, cells, cells, P("wa", "ha")),
        check_vma=False,
    )
```

```python
import functools
import math

import jax
import jax.numpy as jnp
from jax import lax
from jax.experimental import pallas as pl
from jax.experimental.pallas import tpu as pltpu
from jax.sharding import PartitionSpec as P

MESH = pl.DeviceIdType.MESH
TALLS = (6, 8, 12)
BATCH = 3
CHUNKS = 4
HIDDEN = -1e30
FRAME_KINDS = ((1, 0), (1, 1), (1, 2), (2, 0), (2, 1))


def split(low, high):
    count = high - low
    runs = -(-count // BATCH)
    out = []
    for at in range(runs):
        size = count // runs + (1 if at < count % runs else 0)
        out.append((low, size))
        low += size
    return out


def attention_kernel(
    tall_count,
    window_hbm,
    q_ref,
    do_ref,
    k_ref,
    v_ref,
    x_ref,
    att_ref,
    dk_ref,
    dv_ref,
    weight_ref,
    window_ref,
    order_ref,
    pos_ref,
    kind_ref,
    code_ref,
    heads_kv,
    heads_q,
    heads_do,
    padded,
    terms,
    att_slots,
    dq_slots,
    from_side,
    from_row,
    relay_rows,
    relay_terms,
    slopes_own,
    x_all,
    slopes_all,
    product,
    from_partner,
    pair_sums,
    from_pair,
    chip_sums,
    from_chips,
    window_sem,
    row_send,
    row_recv,
    relay_send,
    relay_recv,
    col_send,
    col_recv,
    corner_send,
    corner_recv,
    side_send,
    side_recv,
    x_send,
    x_recv,
    forward_send,
    slope_send,
    slope_recv,
    core_send,
    core_recv,
    pair_send,
    pair_recv,
    chip_send,
    chip_recv,
):
    rows, columns, frames, _ = k_ref.shape
    head_count = padded.shape[0]
    head_size = padded.shape[-1]
    queries = rows * columns * frames
    bf = jnp.bfloat16
    scale = 1.0 / math.sqrt(head_size)
    ha_count, wa_count = lax.axis_size("ha"), lax.axis_size("wa")
    ha, wa = lax.axis_index("ha"), lax.axis_index("wa")
    flat_count = head_count - tall_count
    flat_runs = split(0, flat_count)
    tall_runs = split(flat_count, head_count)
    runs = flat_runs + tall_runs
    place = {"ha": ha, "wa": wa}
    exists = {
        ("ha", -1): ha > 0,
        ("ha", 1): ha < ha_count - 1,
        ("wa", -1): wa > 0,
        ("wa", 1): wa < wa_count - 1,
    }
    above, below = rows, rows + 1
    left, right = columns, columns + 1
    low, high = ha % 2, ha // 2
    partner = 2 * high + 1 - low
    pairs = ha_count // 2
    relayed = pairs == 2

    window_copy = pltpu.make_async_copy(window_hbm, window_ref, window_sem.at[0])
    window_copy.start()
    tall_slots = pl.ds(flat_count, tall_count)
    for at, side, line in ((0, 0, above), (ha_count - 1, 1, below)):

        @pl.when(ha == at)
        def _(side=side, line=line):
            hidden = padded.at[tall_slots, :, line]
            hidden[...] = jnp.zeros(hidden.shape, bf)
            from_row[side] = jnp.zeros(from_row.shape[1:], bf)

    for at, side, line in ((0, 0, left), (wa_count - 1, 1, right)):

        @pl.when(wa == at)
        def _(side=side, line=line):
            for count, first, lines in (
                (flat_count, 0, rows),
                (tall_count, flat_count, rows + 2),
            ):
                if count:
                    hidden = padded.at[pl.ds(first, count), :, pl.ds(0, lines), line]
                    hidden[...] = jnp.zeros(hidden.shape, bf)
                    fold = from_side.at[side, pl.ds(first, count), :, pl.ds(0, lines)]
                    fold[...] = jnp.zeros(fold.shape, bf)

    barrier = pltpu.get_barrier_semaphore()
    for axis, count in (("ha", ha_count), ("wa", wa_count)):
        for step in range(1, count):
            pl.semaphore_signal(
                barrier,
                inc=1,
                device_id={axis: (place[axis] + step) % count},
                device_id_type=MESH,
            )

    for head in range(head_count):
        lanes = slice(head * head_size, (head + 1) * head_size)
        heads_kv[head, 0] = k_ref[:, :, :, lanes]
        heads_kv[head, 1] = v_ref[:, :, :, lanes]
    window_copy.wait()

    reach = [window_ref[2, head] for head in range(head_count)]
    next_tall = head_count - sum(reach)
    next_flat = 0
    spots = []
    for head in range(head_count):
        spot = jnp.where(reach[head] > 0, next_tall, next_flat)
        next_tall = next_tall + reach[head]
        next_flat = next_flat + 1 - reach[head]
        pos_ref[head] = spot
        spots.append(spot)
    kinds = []
    for head in range(head_count):
        tile = jnp.where(window_ref[0, head] == 2, 3, 0) + window_ref[1, head]
        kinds.append(4 * tile + 2 * reach[head] + window_ref[3, head])
    for slot in range(head_count):
        here = [spots[head] == slot for head in range(head_count)]
        order_ref[slot] = sum(jnp.where(here[head], head, 0) for head in range(head_count))
        kind_ref[slot] = sum(jnp.where(here[head], kinds[head], 0) for head in range(head_count))

    for slot in range(head_count):
        padded[slot, :, :rows, :columns] = heads_kv[order_ref[slot]]

    pl.semaphore_wait(barrier, ha_count + wa_count - 2)

    def remote(source, target, send, recv, axis, device):
        return pltpu.make_async_remote_copy(
            src_ref=source,
            dst_ref=target,
            send_sem=send,
            recv_sem=recv,
            device_id={axis: device},
            device_id_type=MESH,
        )

    def landed(buffer, sem):
        pltpu.make_async_copy(buffer, buffer, sem).wait()

    def detour(by):
        if not relayed:
            return None
        return ha == (1 if by > 0 else pairs)

    def row_source(kind, by, part, run):
        first, size = tall_runs[run]
        if kind == 0:
            return padded.at[
                pl.ds(first, size), part, 0 if by < 0 else rows - 1, pl.ds(0, columns)
            ]
        return terms.at[
            pl.ds(first, size), part, above if by < 0 else below, pl.ds(0, columns)
        ]

    def row_target(kind, by, part, run):
        first, size = tall_runs[run]
        if kind == 0:
            return padded.at[
                pl.ds(first, size), part, below if by < 0 else above, pl.ds(0, columns)
            ]
        return from_row.at[1 if by < 0 else 0, pl.ds(first - flat_count, size), part]

    def relay_buffer(kind, run):
        first, size = tall_runs[run]
        return (relay_rows, relay_terms)[kind].at[pl.ds(first - flat_count, size)]

    def row_copy(kind, by, part, run):
        side = 0 if by < 0 else 1
        return remote(
            row_source(kind, by, part, run),
            row_target(kind, by, part, run),
            row_send.at[kind, side, part, run],
            row_recv.at[kind, side, part, run],
            "ha",
            ha + by,
        )

    def detour_copy(kind, by, run):
        side = 0 if by < 0 else 1
        return remote(
            row_source(kind, by, 1, run),
            relay_buffer(kind, run),
            row_send.at[kind, side, 1, run],
            relay_recv.at[kind, run],
            "ha",
            (ha + 2) % ha_count,
        )

    def relay_copy(kind, by, run):
        side = 0 if by < 0 else 1
        return remote(
            relay_buffer(kind, run),
            row_target(kind, by, 1, run),
            relay_send.at[kind, run],
            row_recv.at[kind, side, 1, run],
            "ha",
            partner,
        )

    def each_row_copy(kind, run, act):
        for by in (-1, 1):
            turn = detour(by)
            for part in range(2):
                direct = exists["ha", by]
                if part == 1 and turn is not None:
                    direct = direct & jnp.logical_not(turn)

                    @pl.when(turn)
                    def _(by=by):
                        act(detour_copy(kind, by, run))

                @pl.when(direct)
                def _(by=by, part=part):
                    act(row_copy(kind, by, part, run))

    def start_rows(kind, run):
        each_row_copy(kind, run, lambda copy: copy.start())

    def relay(kind, run):
        if relayed:
            for at, by in ((0, -1), (ha_count - 1, 1)):

                @pl.when(ha == at)
                def _(by=by):
                    landed(relay_buffer(kind, run), relay_recv.at[kind, run])
                    relay_copy(kind, by, run).start()

    def rows_arrived(kind, run):
        for by in (-1, 1):

            @pl.when(exists["ha", -by])
            def _(by=by):
                for part in range(2):
                    row_copy(kind, by, part, run).wait_recv()

    def column_copy(kind, by, run):
        first, size = (tall_runs if kind == 1 else runs)[run]
        slots = pl.ds(first, size)
        side = 0 if by < 0 else 1
        if kind == 2:
            lines = pl.ds(0, rows if first < flat_count else rows + 2)
            source = terms.at[slots, :, lines, left if by < 0 else right]
            target = from_side.at[1 if by < 0 else 0, slots, :, lines]
        else:
            lines = pl.ds(0, rows) if kind == 0 else pl.ds(rows, 2)
            source = padded.at[slots, :, lines, 0 if by < 0 else columns - 1]
            target = padded.at[slots, :, lines, right if by < 0 else left]
        send = (col_send, corner_send, side_send)[kind]
        recv = (col_recv, corner_recv, side_recv)[kind]
        return remote(source, target, send.at[side, run], recv.at[side, run], "wa", wa + by)

    def start_columns(kind, run):
        for by in (-1, 1):

            @pl.when(exists["wa", by])
            def _(by=by):
                column_copy(kind, by, run).start()

    def columns_arrived(kind, run):
        for by in (-1, 1):

            @pl.when(exists["wa", -by])
            def _(by=by):
                column_copy(kind, by, run).wait_recv()

    chunk = queries // CHUNKS

    def x_copy(peer, part):
        tokens = pl.ds(part * chunk, chunk)
        return remote(
            x_all.at[ha, tokens],
            x_all.at[ha, tokens],
            x_send.at[peer, part],
            x_recv.at[ha, part],
            "ha",
            peer,
        )

    last = CHUNKS - 1

    def back_copy(pair):
        tokens = pl.ds(last * chunk, chunk)
        return remote(
            x_all.at[2 * pair + low, tokens],
            x_all.at[2 * pair + low, tokens],
            forward_send.at[pair, last],
            x_recv.at[2 * pair + low, last],
            "ha",
            partner,
        )

    def forward_copy(pair, part):
        tokens = pl.ds(part * chunk, chunk)
        return remote(
            x_all.at[partner, tokens],
            x_all.at[partner, tokens],
            forward_send.at[pair, part],
            x_recv.at[partner, part],
            "ha",
            2 * pair + low,
        )

    def x_landed(peer, part):
        tokens = pl.ds(part * chunk, chunk)
        landed(x_all.at[peer, tokens], x_recv.at[peer, part])

    def other_pairs(act):
        for pair in range(pairs):

            @pl.when(pair != high)
            def _(pair=pair):
                act(pair)

    for run in range(len(tall_runs)):
        start_rows(0, run)
    start_columns(0, 0)
    for at in range(x_ref.shape[3] // head_size):
        lanes = slice(at * head_size, (at + 1) * head_size)
        x_all[ha, :, lanes] = x_ref[:, :, :, lanes].reshape(queries, head_size)
    for run in range(1, len(runs)):
        start_columns(0, run)
    for part in range(CHUNKS):
        other_pairs(lambda pair: x_copy(2 * pair + low, part).start())

    query_id = lax.broadcasted_iota(jnp.int32, (1, queries), 1)
    key_id = lax.broadcasted_iota(jnp.int32, (code_ref.shape[0], 1), 0)
    query_frame = query_id // (rows * columns)
    query_row = (query_id // columns) % rows
    query_column = query_id % columns
    key_frame = key_id % frames
    key_row = key_id // (frames * (columns + 2))
    key_column = (key_id // frames) % (columns + 2)
    key_row = jnp.where(key_row == above, -1, jnp.where(key_row == below, rows, key_row))
    key_column = jnp.where(
        key_column == left, -1, jnp.where(key_column == right, columns, key_column)
    )
    outside = (
        (key_row + ha * rows < 0)
        | (key_row + ha * rows >= ha_count * rows)
        | (key_column + wa * columns < 0)
        | (key_column + wa * columns >= wa_count * columns)
    )
    key_row = jnp.where(outside, 1000, key_row)
    row_gap = jnp.abs(query_row - key_row)
    column_gap = jnp.abs(query_column - key_column)
    cells = jnp.zeros(code_ref.shape, jnp.int32)
    for row_reach in range(2):
        for column_reach in range(2):
            near = (row_gap <= row_reach) & (column_gap <= column_reach)
            cells = cells | jnp.where(near, 1 << (2 * row_reach + column_reach), 0)
    code = jnp.zeros(code_ref.shape, jnp.int32)
    for kind, (tile, frame_reach) in enumerate(FRAME_KINDS):
        gap = jnp.abs(query_frame // tile - key_frame // tile)
        code = code | jnp.where(gap <= frame_reach, cells << (4 * kind), 0)
    code_ref[...] = code
    for head in range(head_count):
        lanes = slice(head * head_size, (head + 1) * head_size)
        heads_q[head] = q_ref[:, :, :, lanes].reshape(queries, head_size)
        heads_do[head] = do_ref[:, :, :, lanes].reshape(queries, head_size)

    across = (((1,), (1,)), ((), ()))
    down = (((0,), (0,)), ((), ()))
    dot = functools.partial(lax.dot_general, preferred_element_type=jnp.float32)
    lift = scale * math.log2(math.e)

    def attend(run):
        first, size = runs[run]
        lines = rows if first < flat_count else rows + 2
        keys = lines * (columns + 2) * frames
        slots = range(first, first + size)
        q = [heads_q[order_ref[slot]] for slot in slots]
        do = [heads_do[order_ref[slot]] for slot in slots]
        k = [padded[slot, 0, :lines].reshape(keys, head_size) for slot in slots]
        v = [padded[slot, 1, :lines].reshape(keys, head_size) for slot in slots]
        bits = [jnp.left_shift(1, kind_ref[slot]) for slot in slots]
        each = range(size)
        scores = [dot(k[i], q[i], across) for i in each]
        upstream = [dot(v[i], do[i], across) for i in each]
        scores = [
            jnp.where((code_ref[:keys] & bits[i]) != 0, scores[i], HIDDEN) for i in each
        ]
        top = [jnp.max(scores[i], axis=0, keepdims=True) for i in each]
        lifted = [jnp.exp2((scores[i] - top[i]) * lift) for i in each]
        total = [jnp.sum(lifted[i], axis=0, keepdims=True) for i in each]
        weight = [(lifted[i] * (1.0 / total[i])).astype(bf) for i in each]
        wide = [weight[i].astype(jnp.float32) for i in each]
        delta = [jnp.sum(wide[i] * upstream[i], axis=0, keepdims=True) for i in each]
        slopes = [(wide[i] * (upstream[i] - delta[i])).astype(bf) for i in each]
        shape = (lines,) + terms.shape[3:]
        for i, slot in enumerate(slots):
            dv = jnp.dot(weight[i], do[i], preferred_element_type=jnp.float32)
            terms[slot, 1, :lines] = dv.astype(bf).reshape(shape)
            dk = jnp.dot(slopes[i], q[i], preferred_element_type=jnp.float32) * scale
            terms[slot, 0, :lines] = dk.astype(bf).reshape(shape)
            att_slots[slot] = dot(weight[i], v[i], down).astype(bf)
            dq_slots[slot] = (dot(slopes[i], k[i], down) * scale).astype(bf)

    tall_base = len(flat_runs)
    opened = 0

    def open_tall(run):
        relay(0, run)
        rows_arrived(0, run)
        start_columns(1, run)

    def pass_on(part):
        x_landed(partner, part)
        other_pairs(lambda pair: forward_copy(pair, part).start())

    passed = 0
    for run in range(len(runs)):
        columns_arrived(0, run)
        if run >= tall_base:
            while opened < min(run - tall_base + 2, len(tall_runs)):
                open_tall(opened)
                opened += 1
            columns_arrived(1, run - tall_base)
        attend(run)
        start_columns(2, run)
        if run < CHUNKS:
            x_copy(partner, run).start()
        if run < tall_base and opened < len(tall_runs):
            open_tall(opened)
            opened += 1
        if run >= 2 and passed < last:
            pass_on(passed)
            passed += 1
    for part in range(len(runs), CHUNKS):
        x_copy(partner, part).start()

    unit = slopes_own.shape[2]
    share = slopes_all.shape[1]
    pieces = head_size // unit
    for head in range(head_count):
        value = dq_slots[pos_ref[head]]
        for piece in range(pieces):
            slopes_own[head * pieces + piece] = value[:, piece * unit : (piece + 1) * unit]

    def slope_copy(peer):
        return remote(
            slopes_own.at[pl.ds(peer * share, share)],
            slopes_all.at[ha],
            slope_send.at[peer],
            slope_recv.at[ha],
            "ha",
            peer,
        )

    for peer in range(ha_count):

        @pl.when(peer != ha)
        def _(peer=peer):
            slope_copy(peer).start()

        @pl.when(peer == ha)
        def _(peer=peer):
            slopes_all[peer] = slopes_own[pl.ds(peer * share, share)]

    for part in range(passed, last):
        pass_on(part)

    def back(pair):
        x_landed(2 * pair + low, last)
        back_copy(pair).start()

    other_pairs(back)
    x_landed(partner, last)

    for head in range(head_count):
        att_ref[:, head * head_size : (head + 1) * head_size] = att_slots[pos_ref[head]]

    def fold_sides(run):
        first, size = runs[run]
        slots = pl.ds(first, size)
        lines = rows if first < flat_count else rows + 2
        columns_arrived(2, run)
        for side, line in ((0, 0), (1, columns - 1)):
            terms[slots, :, :lines, line] = (
                terms[slots, :, :lines, line] + from_side[side, slots, :, :lines]
            )

    for run in range(len(runs)):
        fold_sides(run)

    for peer in range(ha_count):

        @pl.when(peer != ha)
        def _(peer=peer):
            landed(slopes_all.at[peer], slope_recv.at[peer])

    def wait_others(pair):
        for part in range(CHUNKS):
            if part < last:
                x_landed(2 * pair + low, part)
            x_landed(2 * pair + 1 - low, part)

    other_pairs(wait_others)

    core, chip = wa % 2, wa // 2
    chips = wa_count // 2
    halves = chips // 2
    parity, own_half = chip % 2, chip // 2
    block = x_all.shape[2] // chips
    tokens = ha_count * queries
    aligned = block % 128 == 0

    def core_copy(dest):
        return remote(
            product.at[dest, 1 - core],
            from_partner.at[dest],
            core_send.at[dest],
            core_recv.at[dest],
            "wa",
            wa + 1 - 2 * core,
        )

    def pair_copy(half):
        return remote(
            pair_sums.at[2 * half + 1 - parity],
            from_pair.at[half],
            pair_send.at[half],
            pair_recv.at[half],
            "wa",
            2 * (chip + 1 - 2 * parity) + core,
        )

    def chip_copy(half):
        return remote(
            chip_sums.at[half],
            from_chips.at[own_half],
            chip_send.at[half],
            chip_recv.at[own_half],
            "wa",
            2 * (2 * half + parity) + core,
        )

    others = [lax.rem(own_half + 1 + step, halves) for step in range(halves - 1)]
    columns_of = [slopes_all[:, at].reshape(tokens, unit) for at in range(share)]
    slope_block = columns_of[0] if share == 1 else jnp.concatenate(columns_of, axis=1)

    def form_product(dest):
        if aligned:
            lanes = pl.ds(pl.multiple_of(dest * block, block), block)
        else:
            lanes = slice(dest * block, (dest + 1) * block)
        value = dot(x_all[:, :, lanes].reshape(tokens, block), slope_block, down)
        product[dest] = value.astype(bf).reshape(product.shape[1:])
        core_copy(dest).start()

    def wide(value):
        return value.astype(jnp.float32)

    def core_sum(dest):
        core_copy(dest).wait_recv()
        pair_sums[dest] = (wide(product[dest, core]) + wide(from_partner[dest])).astype(bf)

    def chip_sum(half):
        pair_copy(half).wait_recv()
        total = wide(pair_sums[2 * half + parity]) + wide(from_pair[half])
        chip_sums[half] = total.astype(bf)

    if aligned:
        for half in others + [own_half]:
            form_product(2 * half + 1 - parity)
            form_product(2 * half + parity)
    else:
        for dest in range(chips):
            form_product(dest)
    for half in others:
        core_sum(2 * half + 1 - parity)
        pair_copy(half).start()
        core_sum(2 * half + parity)
    for run in range(len(tall_runs)):
        start_rows(1, run)
    for half in others:
        chip_sum(half)
        chip_copy(half).start()
    core_sum(2 * own_half + 1 - parity)
    pair_copy(own_half).start()
    core_sum(2 * own_half + parity)
    for run in range(len(tall_runs)):
        relay(1, run)
    chip_sum(own_half)
    from_chips[own_half] = chip_sums[own_half]

    for run in range(len(tall_runs)):
        rows_arrived(1, run)
        first, size = tall_runs[run]
        slots = pl.ds(first, size)
        near = pl.ds(first - flat_count, size)
        for side, line in ((0, 0), (1, rows - 1)):
            terms[slots, :, line, :columns] = (
                terms[slots, :, line, :columns] + from_row[side, near]
            )

    for head in range(head_count):
        here = slice(head * head_size, (head + 1) * head_size)
        dk_ref[:, :, :, here] = terms[pos_ref[head], 0, :rows, :columns]
        dv_ref[:, :, :, here] = terms[pos_ref[head], 1, :rows, :columns]

    for half in others:
        landed(from_chips.at[half], chip_recv.at[half])
    gathered = from_chips[0].astype(jnp.float32)
    for half in range(1, halves):
        gathered = gathered + from_chips[half].astype(jnp.float32)
    weight_ref[...] = gathered

    for kind in range(2):
        for run in range(len(tall_runs)):
            each_row_copy(kind, run, lambda copy: copy.wait_send())
            if relayed:
                for at, by in ((0, -1), (ha_count - 1, 1)):

                    @pl.when(ha == at)
                    def _(by=by, kind=kind, run=run):
                        relay_copy(kind, by, run).wait_send()

    for kind, count in ((0, len(runs)), (1, len(tall_runs)), (2, len(runs))):
        for run in range(count):
            for by in (-1, 1):

                @pl.when(exists["wa", by])
                def _(by=by, kind=kind, run=run):
                    column_copy(kind, by, run).wait_send()

    def x_sent(pair):
        for part in range(CHUNKS):
            x_copy(2 * pair + low, part).wait_send()
            (forward_copy(pair, part) if part < last else back_copy(pair)).wait_send()

    for part in range(CHUNKS):
        x_copy(partner, part).wait_send()
    other_pairs(x_sent)
    for peer in range(ha_count):

        @pl.when(peer != ha)
        def _(peer=peer):
            slope_copy(peer).wait_send()

    for dest in range(chips):
        core_copy(dest).wait_send()
    for half in range(halves):
        pair_copy(half).wait_send()
    for half in others:
        chip_copy(half).wait_send()


def on_device(
    which, inputs, query_vectors, key_vectors, value_vectors, output_cotangent, window
):
    tall_count = TALLS[which]
    frames, rows, columns, feature = query_vectors.shape
    head_count = window.shape[0]
    head_size = feature // head_count
    queries = frames * rows * columns
    bf = jnp.bfloat16

    def cells(x):
        return x.transpose(1, 2, 0, 3)

    ha_count, wa_count = lax.axis_size("ha"), lax.axis_size("wa")
    chips = wa_count // 2
    halves = chips // 2
    slice_rows = inputs.shape[3] // wa_count
    slice_columns = feature // ha_count
    unit = math.gcd(head_size, slice_columns)
    cell = (frames, head_size)
    tall = (head_count, 2, rows + 2, columns + 2) + cell
    keys = (rows + 2) * (columns + 2) * frames
    part = (slice_rows, slice_columns)
    tall_runs = len(split(head_count - tall_count, head_count))
    runs = len(split(0, head_count - tall_count)) + tall_runs
    vmem = pl.BlockSpec(memory_space=pltpu.VMEM)
    dma = pltpu.SemaphoreType.DMA
    buffers = [
        pltpu.VMEM((keys, queries), jnp.int32),
        pltpu.VMEM((head_count, 2, rows, columns) + cell, bf),
        pltpu.VMEM((head_count, queries, head_size), bf),
        pltpu.VMEM((head_count, queries, head_size), bf),
        pltpu.VMEM(tall, bf),
        pltpu.VMEM(tall, bf),
        pltpu.VMEM((head_count, queries, head_size), bf),
        pltpu.VMEM((head_count, queries, head_size), bf),
        pltpu.VMEM((2, head_count, 2, rows + 2) + cell, bf),
        pltpu.VMEM((2, tall_count, 2, columns) + cell, bf),
        pltpu.VMEM((tall_count, columns) + cell, bf),
        pltpu.VMEM((tall_count, columns) + cell, bf),
        pltpu.VMEM((feature // unit, queries, unit), bf),
        pltpu.VMEM((ha_count, queries, inputs.shape[3]), bf),
        pltpu.VMEM((ha_count, slice_columns // unit, queries, unit), bf),
        pltpu.VMEM((chips, 2) + part, bf),
        pltpu.VMEM((chips,) + part, bf),
        pltpu.VMEM((chips,) + part, bf),
        pltpu.VMEM((halves,) + part, bf),
        pltpu.VMEM((halves,) + part, bf),
        pltpu.VMEM((halves,) + part, bf),
    ]
    held = sum(
        math.prod(buffer.shape) * jnp.dtype(buffer.dtype).itemsize for buffer in buffers
    )
    held += 10 * queries * feature * 2
    att, dk, dv, weight_gradient = pl.pallas_call(
        functools.partial(attention_kernel, tall_count),
        out_shape=(
            jax.ShapeDtypeStruct((queries, feature), bf),
            jax.ShapeDtypeStruct((rows, columns, frames, feature), bf),
            jax.ShapeDtypeStruct((rows, columns, frames, feature), bf),
            jax.ShapeDtypeStruct(part, jnp.float32),
        ),
        in_specs=[pl.BlockSpec(memory_space=pl.ANY), vmem, vmem, vmem, vmem, vmem],
        out_specs=(vmem, vmem, vmem, vmem),
        scratch_shapes=[
            pltpu.SMEM(window.shape[::-1], window.dtype),
            pltpu.SMEM((head_count,), jnp.int32),
            pltpu.SMEM((head_count,), jnp.int32),
            pltpu.SMEM((head_count,), jnp.int32),
            *buffers,
            dma((1,)),
            dma((2, 2, 2, tall_runs)),
            dma((2, 2, 2, tall_runs)),
            dma((2, tall_runs)),
            dma((2, tall_runs)),
            dma((2, runs)),
            dma((2, runs)),
            dma((2, tall_runs)),
            dma((2, tall_runs)),
            dma((2, runs)),
            dma((2, runs)),
            dma((ha_count, CHUNKS)),
            dma((ha_count, CHUNKS)),
            dma((ha_count // 2, CHUNKS)),
            dma((ha_count,)),
            dma((ha_count,)),
            dma((chips,)),
            dma((chips,)),
            dma((halves,)),
            dma((halves,)),
            dma((halves,)),
            dma((halves,)),
        ],
        compiler_params=pltpu.CompilerParams(
            collective_id=which, has_side_effects=True, vmem_limit_bytes=held + 2 * 1024 * 1024
        ),
    )(
        window.T,
        query_vectors,
        output_cotangent,
        cells(key_vectors),
        cells(value_vectors),
        inputs,
    )

    tokens_all = queries * ha_count * wa_count
    weight_gradient = (weight_gradient * (1.0 / math.sqrt(tokens_all))).astype(bf)

    def to_grid(x):
        return x.transpose(2, 0, 1, 3)

    return (att.reshape(query_vectors.shape), to_grid(dk), to_grid(dv), weight_gradient)


def by_reach(*args):
    reaching = jnp.sum(args[5][:, 2])
    which = sum((reaching > most).astype(jnp.int32) for most in TALLS[:-1])
    branches = [functools.partial(on_device, at) for at in range(len(TALLS))]
    return lax.switch(which, branches, *args)


def solution(mesh):
    cells = P(None, "ha", "wa", None)
    return jax.shard_map(
        by_reach,
        mesh=mesh,
        in_specs=(cells, cells, cells, cells, cells, P()),
        out_specs=(cells, cells, cells, P("wa", "ha")),
        check_vma=False,
    )
```

```python
import functools
import math

import jax
import jax.numpy as jnp
from jax import lax
from jax.experimental import pallas as pl
from jax.experimental.pallas import tpu as pltpu
from jax.sharding import PartitionSpec as P

MESH = pl.DeviceIdType.MESH
TALLS = (6, 8, 12)
BATCH = 3
CHUNKS = 4
HIDDEN = -1e30
FRAME_KINDS = ((1, 0), (1, 1), (1, 2), (2, 0), (2, 1))


def split(low, high):
    count = high - low
    runs = -(-count // BATCH)
    out = []
    for at in range(runs):
        size = count // runs + (1 if at < count % runs else 0)
        out.append((low, size))
        low += size
    return out


def attention_kernel(
    tall_count,
    window_hbm,
    q_ref,
    do_ref,
    k_ref,
    v_ref,
    x_ref,
    att_ref,
    dk_ref,
    dv_ref,
    weight_ref,
    window_ref,
    order_ref,
    pos_ref,
    kind_ref,
    code_ref,
    heads_kv,
    heads_q,
    heads_do,
    padded,
    terms,
    att_slots,
    dq_slots,
    from_side,
    from_row,
    relay_rows,
    relay_terms,
    slopes_own,
    x_all,
    slopes_all,
    product,
    from_partner,
    pair_sums,
    from_pair,
    chip_sums,
    from_chips,
    window_sem,
    row_send,
    row_recv,
    relay_send,
    relay_recv,
    col_send,
    col_recv,
    corner_send,
    corner_recv,
    side_send,
    side_recv,
    x_send,
    x_recv,
    forward_send,
    slope_send,
    slope_recv,
    core_send,
    core_recv,
    pair_send,
    pair_recv,
    chip_send,
    chip_recv,
):
    rows, columns, frames, _ = k_ref.shape
    head_count = padded.shape[0]
    head_size = padded.shape[-1]
    queries = rows * columns * frames
    bf = jnp.bfloat16
    scale = 1.0 / math.sqrt(head_size)
    ha_count, wa_count = lax.axis_size("ha"), lax.axis_size("wa")
    ha, wa = lax.axis_index("ha"), lax.axis_index("wa")
    flat_count = head_count - tall_count
    flat_runs = split(0, flat_count)
    tall_runs = split(flat_count, head_count)
    runs = flat_runs + tall_runs
    place = {"ha": ha, "wa": wa}
    exists = {
        ("ha", -1): ha > 0,
        ("ha", 1): ha < ha_count - 1,
        ("wa", -1): wa > 0,
        ("wa", 1): wa < wa_count - 1,
    }
    above, below = rows, rows + 1
    left, right = columns, columns + 1
    low, high = ha % 2, ha // 2
    partner = 2 * high + 1 - low
    pairs = ha_count // 2
    relayed = pairs == 2

    window_copy = pltpu.make_async_copy(window_hbm, window_ref, window_sem.at[0])
    window_copy.start()
    tall_slots = pl.ds(flat_count, tall_count)
    for at, side, line in ((0, 0, above), (ha_count - 1, 1, below)):

        @pl.when(ha == at)
        def _(side=side, line=line):
            hidden = padded.at[tall_slots, :, line]
            hidden[...] = jnp.zeros(hidden.shape, bf)
            from_row[side] = jnp.zeros(from_row.shape[1:], bf)

    for at, side, line in ((0, 0, left), (wa_count - 1, 1, right)):

        @pl.when(wa == at)
        def _(side=side, line=line):
            for count, first, lines in (
                (flat_count, 0, rows),
                (tall_count, flat_count, rows + 2),
            ):
                if count:
                    hidden = padded.at[pl.ds(first, count), :, pl.ds(0, lines), line]
                    hidden[...] = jnp.zeros(hidden.shape, bf)
                    fold = from_side.at[side, pl.ds(first, count), :, pl.ds(0, lines)]
                    fold[...] = jnp.zeros(fold.shape, bf)

    barrier = pltpu.get_barrier_semaphore()
    for axis, count in (("ha", ha_count), ("wa", wa_count)):
        for step in range(1, count):
            pl.semaphore_signal(
                barrier,
                inc=1,
                device_id={axis: (place[axis] + step) % count},
                device_id_type=MESH,
            )

    for head in range(head_count):
        lanes = slice(head * head_size, (head + 1) * head_size)
        heads_kv[head, 0] = k_ref[:, :, :, lanes]
        heads_kv[head, 1] = v_ref[:, :, :, lanes]
    window_copy.wait()

    reach = [window_ref[2, head] for head in range(head_count)]
    next_tall = head_count - sum(reach)
    next_flat = 0
    spots = []
    for head in range(head_count):
        spot = jnp.where(reach[head] > 0, next_tall, next_flat)
        next_tall = next_tall + reach[head]
        next_flat = next_flat + 1 - reach[head]
        pos_ref[head] = spot
        spots.append(spot)
    kinds = []
    for head in range(head_count):
        tile = jnp.where(window_ref[0, head] == 2, 3, 0) + window_ref[1, head]
        kinds.append(4 * tile + 2 * reach[head] + window_ref[3, head])
    for slot in range(head_count):
        here = [spots[head] == slot for head in range(head_count)]
        order_ref[slot] = sum(jnp.where(here[head], head, 0) for head in range(head_count))
        kind_ref[slot] = sum(jnp.where(here[head], kinds[head], 0) for head in range(head_count))

    for slot in range(head_count):
        padded[slot, :, :rows, :columns] = heads_kv[order_ref[slot]]

    pl.semaphore_wait(barrier, ha_count + wa_count - 2)

    def remote(source, target, send, recv, axis, device):
        return pltpu.make_async_remote_copy(
            src_ref=source,
            dst_ref=target,
            send_sem=send,
            recv_sem=recv,
            device_id={axis: device},
            device_id_type=MESH,
        )

    def landed(buffer, sem):
        pltpu.make_async_copy(buffer, buffer, sem).wait()

    def detour(by):
        if not relayed:
            return None
        return ha == (1 if by > 0 else pairs)

    def row_source(kind, by, part, run):
        first, size = tall_runs[run]
        if kind == 0:
            return padded.at[
                pl.ds(first, size), part, 0 if by < 0 else rows - 1, pl.ds(0, columns)
            ]
        return terms.at[
            pl.ds(first, size), part, above if by < 0 else below, pl.ds(0, columns)
        ]

    def row_target(kind, by, part, run):
        first, size = tall_runs[run]
        if kind == 0:
            return padded.at[
                pl.ds(first, size), part, below if by < 0 else above, pl.ds(0, columns)
            ]
        return from_row.at[1 if by < 0 else 0, pl.ds(first - flat_count, size), part]

    def relay_buffer(kind, run):
        first, size = tall_runs[run]
        return (relay_rows, relay_terms)[kind].at[pl.ds(first - flat_count, size)]

    def row_copy(kind, by, part, run):
        side = 0 if by < 0 else 1
        return remote(
            row_source(kind, by, part, run),
            row_target(kind, by, part, run),
            row_send.at[kind, side, part, run],
            row_recv.at[kind, side, part, run],
            "ha",
            ha + by,
        )

    def detour_copy(kind, by, run):
        side = 0 if by < 0 else 1
        return remote(
            row_source(kind, by, 1, run),
            relay_buffer(kind, run),
            row_send.at[kind, side, 1, run],
            relay_recv.at[kind, run],
            "ha",
            (ha + 2) % ha_count,
        )

    def relay_copy(kind, by, run):
        side = 0 if by < 0 else 1
        return remote(
            relay_buffer(kind, run),
            row_target(kind, by, 1, run),
            relay_send.at[kind, run],
            row_recv.at[kind, side, 1, run],
            "ha",
            partner,
        )

    def each_row_copy(kind, run, act):
        for by in (-1, 1):
            turn = detour(by)
            for part in range(2):
                direct = exists["ha", by]
                if part == 1 and turn is not None:
                    direct = direct & jnp.logical_not(turn)

                    @pl.when(turn)
                    def _(by=by):
                        act(detour_copy(kind, by, run))

                @pl.when(direct)
                def _(by=by, part=part):
                    act(row_copy(kind, by, part, run))

    def start_rows(kind, run):
        each_row_copy(kind, run, lambda copy: copy.start())

    def relay(kind, run):
        if relayed:
            for at, by in ((0, -1), (ha_count - 1, 1)):

                @pl.when(ha == at)
                def _(by=by):
                    landed(relay_buffer(kind, run), relay_recv.at[kind, run])
                    relay_copy(kind, by, run).start()

    def rows_arrived(kind, run):
        for by in (-1, 1):

            @pl.when(exists["ha", -by])
            def _(by=by):
                for part in range(2):
                    row_copy(kind, by, part, run).wait_recv()

    def column_copy(kind, by, run):
        first, size = (tall_runs if kind == 1 else runs)[run]
        slots = pl.ds(first, size)
        side = 0 if by < 0 else 1
        if kind == 2:
            lines = pl.ds(0, rows if first < flat_count else rows + 2)
            source = terms.at[slots, :, lines, left if by < 0 else right]
            target = from_side.at[1 if by < 0 else 0, slots, :, lines]
        else:
            lines = pl.ds(0, rows) if kind == 0 else pl.ds(rows, 2)
            source = padded.at[slots, :, lines, 0 if by < 0 else columns - 1]
            target = padded.at[slots, :, lines, right if by < 0 else left]
        send = (col_send, corner_send, side_send)[kind]
        recv = (col_recv, corner_recv, side_recv)[kind]
        return remote(source, target, send.at[side, run], recv.at[side, run], "wa", wa + by)

    def start_columns(kind, run):
        for by in (-1, 1):

            @pl.when(exists["wa", by])
            def _(by=by):
                column_copy(kind, by, run).start()

    def columns_arrived(kind, run):
        for by in (-1, 1):

            @pl.when(exists["wa", -by])
            def _(by=by):
                column_copy(kind, by, run).wait_recv()

    chunk = queries // CHUNKS

    def x_copy(peer, part):
        tokens = pl.ds(part * chunk, chunk)
        return remote(
            x_all.at[ha, tokens],
            x_all.at[ha, tokens],
            x_send.at[peer, part],
            x_recv.at[ha, part],
            "ha",
            peer,
        )

    last = CHUNKS - 1

    def back_copy(pair):
        tokens = pl.ds(last * chunk, chunk)
        return remote(
            x_all.at[2 * pair + low, tokens],
            x_all.at[2 * pair + low, tokens],
            forward_send.at[pair, last],
            x_recv.at[2 * pair + low, last],
            "ha",
            partner,
        )

    def forward_copy(pair, part):
        tokens = pl.ds(part * chunk, chunk)
        return remote(
            x_all.at[partner, tokens],
            x_all.at[partner, tokens],
            forward_send.at[pair, part],
            x_recv.at[partner, part],
            "ha",
            2 * pair + low,
        )

    def x_landed(peer, part):
        tokens = pl.ds(part * chunk, chunk)
        landed(x_all.at[peer, tokens], x_recv.at[peer, part])

    def other_pairs(act):
        for pair in range(pairs):

            @pl.when(pair != high)
            def _(pair=pair):
                act(pair)

    for run in range(len(tall_runs)):
        start_rows(0, run)
    start_columns(0, 0)
    for at in range(x_ref.shape[3] // head_size):
        lanes = slice(at * head_size, (at + 1) * head_size)
        x_all[ha, :, lanes] = x_ref[:, :, :, lanes].reshape(queries, head_size)
    for run in range(1, len(runs)):
        start_columns(0, run)
    for part in range(CHUNKS):
        other_pairs(lambda pair: x_copy(2 * pair + low, part).start())

    query_id = lax.broadcasted_iota(jnp.int32, (1, queries), 1)
    key_id = lax.broadcasted_iota(jnp.int32, (code_ref.shape[0], 1), 0)
    query_frame = query_id // (rows * columns)
    query_row = (query_id // columns) % rows
    query_column = query_id % columns
    key_frame = key_id % frames
    key_row = key_id // (frames * (columns + 2))
    key_column = (key_id // frames) % (columns + 2)
    key_row = jnp.where(key_row == above, -1, jnp.where(key_row == below, rows, key_row))
    key_column = jnp.where(
        key_column == left, -1, jnp.where(key_column == right, columns, key_column)
    )
    outside = (
        (key_row + ha * rows < 0)
        | (key_row + ha * rows >= ha_count * rows)
        | (key_column + wa * columns < 0)
        | (key_column + wa * columns >= wa_count * columns)
    )
    key_row = jnp.where(outside, 1000, key_row)
    row_gap = jnp.abs(query_row - key_row)
    column_gap = jnp.abs(query_column - key_column)
    cells = jnp.zeros(code_ref.shape, jnp.int32)
    for row_reach in range(2):
        for column_reach in range(2):
            near = (row_gap <= row_reach) & (column_gap <= column_reach)
            cells = cells | jnp.where(near, 1 << (2 * row_reach + column_reach), 0)
    code = jnp.zeros(code_ref.shape, jnp.int32)
    for kind, (tile, frame_reach) in enumerate(FRAME_KINDS):
        gap = jnp.abs(query_frame // tile - key_frame // tile)
        code = code | jnp.where(gap <= frame_reach, cells << (4 * kind), 0)
    code_ref[...] = code
    for head in range(head_count):
        lanes = slice(head * head_size, (head + 1) * head_size)
        heads_q[head] = q_ref[:, :, :, lanes].reshape(queries, head_size)
        heads_do[head] = do_ref[:, :, :, lanes].reshape(queries, head_size)

    across = (((1,), (1,)), ((), ()))
    down = (((0,), (0,)), ((), ()))
    dot = functools.partial(lax.dot_general, preferred_element_type=jnp.float32)
    lift = scale * math.log2(math.e)

    def attend(run):
        first, size = runs[run]
        lines = rows if first < flat_count else rows + 2
        keys = lines * (columns + 2) * frames
        slots = range(first, first + size)
        q = [heads_q[order_ref[slot]] for slot in slots]
        do = [heads_do[order_ref[slot]] for slot in slots]
        k = [padded[slot, 0, :lines].reshape(keys, head_size) for slot in slots]
        v = [padded[slot, 1, :lines].reshape(keys, head_size) for slot in slots]
        bits = [jnp.left_shift(1, kind_ref[slot]) for slot in slots]
        each = range(size)
        scores = [dot(k[i], q[i], across) for i in each]
        upstream = [dot(v[i], do[i], across) for i in each]
        scores = [
            jnp.where((code_ref[:keys] & bits[i]) != 0, scores[i], HIDDEN) for i in each
        ]
        top = [jnp.max(scores[i], axis=0, keepdims=True) for i in each]
        lifted = [jnp.exp2((scores[i] - top[i]) * lift) for i in each]
        total = [jnp.sum(lifted[i], axis=0, keepdims=True) for i in each]
        weight = [(lifted[i] * (1.0 / total[i])).astype(bf) for i in each]
        wide = [weight[i].astype(jnp.float32) for i in each]
        delta = [jnp.sum(wide[i] * upstream[i], axis=0, keepdims=True) for i in each]
        slopes = [(wide[i] * (upstream[i] - delta[i])).astype(bf) for i in each]
        shape = (lines,) + terms.shape[3:]
        for i, slot in enumerate(slots):
            dv = jnp.dot(weight[i], do[i], preferred_element_type=jnp.float32)
            terms[slot, 1, :lines] = dv.astype(bf).reshape(shape)
            dk = jnp.dot(slopes[i], q[i], preferred_element_type=jnp.float32) * scale
            terms[slot, 0, :lines] = dk.astype(bf).reshape(shape)
            att_slots[slot] = dot(weight[i], v[i], down).astype(bf)
            dq_slots[slot] = (dot(slopes[i], k[i], down) * scale).astype(bf)

    tall_base = len(flat_runs)
    opened = 0

    def open_tall(run):
        relay(0, run)
        rows_arrived(0, run)
        start_columns(1, run)

    def pass_on(part):
        x_landed(partner, part)
        other_pairs(lambda pair: forward_copy(pair, part).start())

    passed = 0
    for run in range(len(runs)):
        columns_arrived(0, run)
        if run >= tall_base:
            while opened < min(run - tall_base + 2, len(tall_runs)):
                open_tall(opened)
                opened += 1
            columns_arrived(1, run - tall_base)
        attend(run)
        start_columns(2, run)
        if run < CHUNKS:
            x_copy(partner, run).start()
        if run < tall_base and opened < len(tall_runs):
            open_tall(opened)
            opened += 1
        if run >= 2 and passed < last:
            pass_on(passed)
            passed += 1
    for part in range(len(runs), CHUNKS):
        x_copy(partner, part).start()

    unit = slopes_own.shape[2]
    share = slopes_all.shape[1]
    pieces = head_size // unit
    for head in range(head_count):
        value = dq_slots[pos_ref[head]]
        for piece in range(pieces):
            slopes_own[head * pieces + piece] = value[:, piece * unit : (piece + 1) * unit]

    def slope_copy(peer):
        return remote(
            slopes_own.at[pl.ds(peer * share, share)],
            slopes_all.at[ha],
            slope_send.at[peer],
            slope_recv.at[ha],
            "ha",
            peer,
        )

    for peer in range(ha_count):

        @pl.when(peer != ha)
        def _(peer=peer):
            slope_copy(peer).start()

        @pl.when(peer == ha)
        def _(peer=peer):
            slopes_all[peer] = slopes_own[pl.ds(peer * share, share)]

    for part in range(passed, last):
        pass_on(part)

    def back(pair):
        x_landed(2 * pair + low, last)
        back_copy(pair).start()

    other_pairs(back)
    x_landed(partner, last)

    for head in range(head_count):
        here = slice(head * head_size, (head + 1) * head_size)
        cells = (frames, rows, columns, head_size)
        att_ref[:, :, :, here] = att_slots[pos_ref[head]].reshape(cells)

    def fold_sides(run):
        first, size = runs[run]
        slots = pl.ds(first, size)
        lines = rows if first < flat_count else rows + 2
        columns_arrived(2, run)
        for side, line in ((0, 0), (1, columns - 1)):
            terms[slots, :, :lines, line] = (
                terms[slots, :, :lines, line] + from_side[side, slots, :, :lines]
            )

    for run in range(len(runs)):
        fold_sides(run)

    for peer in range(ha_count):

        @pl.when(peer != ha)
        def _(peer=peer):
            landed(slopes_all.at[peer], slope_recv.at[peer])

    def wait_others(pair):
        for part in range(CHUNKS):
            if part < last:
                x_landed(2 * pair + low, part)
            x_landed(2 * pair + 1 - low, part)

    other_pairs(wait_others)

    core, chip = wa % 2, wa // 2
    chips = wa_count // 2
    halves = chips // 2
    parity, own_half = chip % 2, chip // 2
    block = x_all.shape[2] // chips
    tokens = ha_count * queries
    aligned = block % 128 == 0

    def core_copy(dest):
        return remote(
            product.at[dest, 1 - core],
            from_partner.at[dest],
            core_send.at[dest],
            core_recv.at[dest],
            "wa",
            wa + 1 - 2 * core,
        )

    def pair_copy(half):
        return remote(
            pair_sums.at[2 * half + 1 - parity],
            from_pair.at[half],
            pair_send.at[half],
            pair_recv.at[half],
            "wa",
            2 * (chip + 1 - 2 * parity) + core,
        )

    def chip_copy(half):
        return remote(
            chip_sums.at[half],
            from_chips.at[own_half],
            chip_send.at[half],
            chip_recv.at[own_half],
            "wa",
            2 * (2 * half + parity) + core,
        )

    others = [lax.rem(own_half + 1 + step, halves) for step in range(halves - 1)]
    columns_of = [slopes_all[:, at].reshape(tokens, unit) for at in range(share)]
    slope_block = columns_of[0] if share == 1 else jnp.concatenate(columns_of, axis=1)

    def form_product(dest):
        if aligned:
            lanes = pl.ds(pl.multiple_of(dest * block, block), block)
        else:
            lanes = slice(dest * block, (dest + 1) * block)
        value = dot(x_all[:, :, lanes].reshape(tokens, block), slope_block, down)
        product[dest] = value.astype(bf).reshape(product.shape[1:])
        core_copy(dest).start()

    def wide(value):
        return value.astype(jnp.float32)

    def core_sum(dest):
        core_copy(dest).wait_recv()
        pair_sums[dest] = (wide(product[dest, core]) + wide(from_partner[dest])).astype(bf)

    def chip_sum(half):
        pair_copy(half).wait_recv()
        total = wide(pair_sums[2 * half + parity]) + wide(from_pair[half])
        chip_sums[half] = total.astype(bf)

    if aligned:
        for half in others + [own_half]:
            form_product(2 * half + 1 - parity)
            form_product(2 * half + parity)
    else:
        for dest in range(chips):
            form_product(dest)
    for half in others:
        core_sum(2 * half + 1 - parity)
        pair_copy(half).start()
        core_sum(2 * half + parity)
    for run in range(len(tall_runs)):
        start_rows(1, run)
    for half in others:
        chip_sum(half)
        chip_copy(half).start()
    core_sum(2 * own_half + 1 - parity)
    pair_copy(own_half).start()
    core_sum(2 * own_half + parity)
    for run in range(len(tall_runs)):
        relay(1, run)
    chip_sum(own_half)
    from_chips[own_half] = chip_sums[own_half]

    for run in range(len(tall_runs)):
        rows_arrived(1, run)
        first, size = tall_runs[run]
        slots = pl.ds(first, size)
        near = pl.ds(first - flat_count, size)
        for side, line in ((0, 0), (1, rows - 1)):
            terms[slots, :, line, :columns] = (
                terms[slots, :, line, :columns] + from_row[side, near]
            )

    for head in range(head_count):
        here = slice(head * head_size, (head + 1) * head_size)
        dk_ref[:, :, :, here] = terms[pos_ref[head], 0, :rows, :columns]
        dv_ref[:, :, :, here] = terms[pos_ref[head], 1, :rows, :columns]

    for half in others:
        landed(from_chips.at[half], chip_recv.at[half])
    gathered = from_chips[0].astype(jnp.float32)
    for half in range(1, halves):
        gathered = gathered + from_chips[half].astype(jnp.float32)
    weight_ref[...] = gathered

    for kind in range(2):
        for run in range(len(tall_runs)):
            each_row_copy(kind, run, lambda copy: copy.wait_send())
            if relayed:
                for at, by in ((0, -1), (ha_count - 1, 1)):

                    @pl.when(ha == at)
                    def _(by=by, kind=kind, run=run):
                        relay_copy(kind, by, run).wait_send()

    for kind, count in ((0, len(runs)), (1, len(tall_runs)), (2, len(runs))):
        for run in range(count):
            for by in (-1, 1):

                @pl.when(exists["wa", by])
                def _(by=by, kind=kind, run=run):
                    column_copy(kind, by, run).wait_send()

    def x_sent(pair):
        for part in range(CHUNKS):
            x_copy(2 * pair + low, part).wait_send()
            (forward_copy(pair, part) if part < last else back_copy(pair)).wait_send()

    for part in range(CHUNKS):
        x_copy(partner, part).wait_send()
    other_pairs(x_sent)
    for peer in range(ha_count):

        @pl.when(peer != ha)
        def _(peer=peer):
            slope_copy(peer).wait_send()

    for dest in range(chips):
        core_copy(dest).wait_send()
    for half in range(halves):
        pair_copy(half).wait_send()
    for half in others:
        chip_copy(half).wait_send()


def on_device(
    which, inputs, query_vectors, key_vectors, value_vectors, output_cotangent, window
):
    tall_count = TALLS[which]
    frames, rows, columns, feature = query_vectors.shape
    head_count = window.shape[0]
    head_size = feature // head_count
    queries = frames * rows * columns
    bf = jnp.bfloat16

    def cells(x):
        return x.transpose(1, 2, 0, 3)

    ha_count, wa_count = lax.axis_size("ha"), lax.axis_size("wa")
    chips = wa_count // 2
    halves = chips // 2
    slice_rows = inputs.shape[3] // wa_count
    slice_columns = feature // ha_count
    unit = math.gcd(head_size, slice_columns)
    cell = (frames, head_size)
    tall = (head_count, 2, rows + 2, columns + 2) + cell
    keys = (rows + 2) * (columns + 2) * frames
    part = (slice_rows, slice_columns)
    tall_runs = len(split(head_count - tall_count, head_count))
    runs = len(split(0, head_count - tall_count)) + tall_runs
    vmem = pl.BlockSpec(memory_space=pltpu.VMEM)
    dma = pltpu.SemaphoreType.DMA
    buffers = [
        pltpu.VMEM((keys, queries), jnp.int32),
        pltpu.VMEM((head_count, 2, rows, columns) + cell, bf),
        pltpu.VMEM((head_count, queries, head_size), bf),
        pltpu.VMEM((head_count, queries, head_size), bf),
        pltpu.VMEM(tall, bf),
        pltpu.VMEM(tall, bf),
        pltpu.VMEM((head_count, queries, head_size), bf),
        pltpu.VMEM((head_count, queries, head_size), bf),
        pltpu.VMEM((2, head_count, 2, rows + 2) + cell, bf),
        pltpu.VMEM((2, tall_count, 2, columns) + cell, bf),
        pltpu.VMEM((tall_count, columns) + cell, bf),
        pltpu.VMEM((tall_count, columns) + cell, bf),
        pltpu.VMEM((feature // unit, queries, unit), bf),
        pltpu.VMEM((ha_count, queries, inputs.shape[3]), bf),
        pltpu.VMEM((ha_count, slice_columns // unit, queries, unit), bf),
        pltpu.VMEM((chips, 2) + part, bf),
        pltpu.VMEM((chips,) + part, bf),
        pltpu.VMEM((chips,) + part, bf),
        pltpu.VMEM((halves,) + part, bf),
        pltpu.VMEM((halves,) + part, bf),
        pltpu.VMEM((halves,) + part, bf),
    ]
    held = sum(
        math.prod(buffer.shape) * jnp.dtype(buffer.dtype).itemsize for buffer in buffers
    )
    held += 10 * queries * feature * 2
    att, dk, dv, weight_gradient = pl.pallas_call(
        functools.partial(attention_kernel, tall_count),
        out_shape=(
            jax.ShapeDtypeStruct(query_vectors.shape, bf),
            jax.ShapeDtypeStruct((rows, columns, frames, feature), bf),
            jax.ShapeDtypeStruct((rows, columns, frames, feature), bf),
            jax.ShapeDtypeStruct(part, jnp.float32),
        ),
        in_specs=[pl.BlockSpec(memory_space=pl.ANY), vmem, vmem, vmem, vmem, vmem],
        out_specs=(vmem, vmem, vmem, vmem),
        scratch_shapes=[
            pltpu.SMEM(window.shape[::-1], window.dtype),
            pltpu.SMEM((head_count,), jnp.int32),
            pltpu.SMEM((head_count,), jnp.int32),
            pltpu.SMEM((head_count,), jnp.int32),
            *buffers,
            dma((1,)),
            dma((2, 2, 2, tall_runs)),
            dma((2, 2, 2, tall_runs)),
            dma((2, tall_runs)),
            dma((2, tall_runs)),
            dma((2, runs)),
            dma((2, runs)),
            dma((2, tall_runs)),
            dma((2, tall_runs)),
            dma((2, runs)),
            dma((2, runs)),
            dma((ha_count, CHUNKS)),
            dma((ha_count, CHUNKS)),
            dma((ha_count // 2, CHUNKS)),
            dma((ha_count,)),
            dma((ha_count,)),
            dma((chips,)),
            dma((chips,)),
            dma((halves,)),
            dma((halves,)),
            dma((halves,)),
            dma((halves,)),
        ],
        compiler_params=pltpu.CompilerParams(
            collective_id=which, has_side_effects=True, vmem_limit_bytes=held + 2 * 1024 * 1024
        ),
    )(
        window.T,
        query_vectors,
        output_cotangent,
        cells(key_vectors),
        cells(value_vectors),
        inputs,
    )

    tokens_all = queries * ha_count * wa_count
    weight_gradient = (weight_gradient * (1.0 / math.sqrt(tokens_all))).astype(bf)

    def to_grid(x):
        return x.transpose(2, 0, 1, 3)

    return (att, to_grid(dk), to_grid(dv), weight_gradient)


def by_reach(*args):
    reaching = jnp.sum(args[5][:, 2])
    which = sum((reaching > most).astype(jnp.int32) for most in TALLS[:-1])
    branches = [functools.partial(on_device, at) for at in range(len(TALLS))]
    return lax.switch(which, branches, *args)


def solution(mesh):
    cells = P(None, "ha", "wa", None)
    return jax.shard_map(
        by_reach,
        mesh=mesh,
        in_specs=(cells, cells, cells, cells, cells, P()),
        out_specs=(cells, cells, cells, P("wa", "ha")),
        check_vma=False,
    )
```
